32 devices in a mesh: row: 8 (over z, y), col: 4 (over x, core).
Axes of the slice: x: 2, y: 2, z: 4, core: 2. Of those that a mesh axis runs over, the one named last changes fastest.
Arguments:
- sub_field: float32 [65536, 128], P(('row', 'col')), may hold values from -2.4 to 2.4
- reluctivity: float32 [2, 65536, 128], P(None, ('row', 'col')), may hold values from 0.3 to 3
- stride: int32 [32], P(('row', 'col')), may hold values from 2 to 511
- counts: int32 [32, 8], P(('row', 'col')), may hold values from 1 to 32, as said below
- source_cell: int32 [32, 8, 32], P(('row', 'col')), may hold values from 0 to 2047
- target_row: int32 [8, 4, 8, 32], P('row', 'col'), may hold values from 0 to 2047
- lower_tiles: float32 [28, 2048, 2048], P(None, 'row', 'col'), may hold values from -0.046875 to 0.046875
- diag_inverse: float32 [8, 2048, 2048], P(None, 'col', 'row'), may hold values from -1 to 2, as said below
Outputs:
- solution: float32 [8, 4, 512, 128], P(None, 'col', 'row')
The draws below stay inside these ranges and needn't reach their ends.
Inputs may be any that keep to these rules, and one draw needn't show every extreme that they name: `counts`: every subdomain sends at least one contribution to every grid row; in every draw one grid row receives 32 contributions from every subdomain. `diag_inverse`: block i is the given inverse of the window's diagonal block i.
All inputs are finite; a program needn't handle non-finite values.
Results may differ from the reference program's by a relative error of at most 0.0003.
Values sent between devices are 32-bit elements; how exact they have to be, the bound alone decides.
A program may use at most 128 MiB of HBM per device.

```python
import math
import jax
import jax.numpy as jnp
from jax import lax

R = 128
TB = 256
WIN = 8
SC = 2048
CAP = 32
NB = 2048
CB = 512
PAIRS = 28
NSUB = 32
N_ROW = 8
N_COL = 4


def draw_counts(key, part):
    first_key, second_key = jax.random.split(key)
    hottest = jax.random.randint(first_key, (), 0, N_ROW)
    base_counts = jax.random.randint(second_key, (NSUB, N_ROW), 1, CAP + 1)
    columns = jnp.arange(N_ROW, dtype=jnp.int32)[None, :]
    return jnp.where(columns == hottest, CAP, base_counts).astype(jnp.int32)


def draw_diag_inverse(key, part):
    first_key, second_key = jax.random.split(key)
    rows = jnp.arange(NB, dtype=jnp.int32)[:, None]
    columns = jnp.arange(NB, dtype=jnp.int32)[None, :]
    identity = (rows == columns).astype(jnp.float32)
    spread = jax.random.normal(first_key, (WIN, NB, NB), jnp.float32) * (0.45 / NB ** 0.5)
    diagonal = jax.random.uniform(second_key, (WIN, NB), jnp.float32, 0.8, 1.2)
    return (spread + identity[None, :, :] * diagonal[:, :, None]).astype(jnp.float32)


def plant(entries, stream_key, smallest, top_value):
    longest = entries.shape.index(max(entries.shape))
    spots = []
    for shift in (0, 1):
        where = [jax.random.randint(jax.random.fold_in(stream_key, axis), (), 0, length) for axis, length in enumerate(entries.shape)]
        where[longest] = (where[longest] + shift) % entries.shape[longest]
        spots.append(tuple(where))
    return entries.at[spots[0]].set(smallest).at[spots[1]].set(top_value)


def shard_levels(key, shape, cuts, low, largest):
    def one(axis_at, shards_of):
        steps = jax.random.uniform(jax.random.fold_in(jax.random.fold_in(key, 6), axis_at), (shards_of,), jnp.float32, low / len(cuts), largest / len(cuts))
        return jnp.repeat(jnp.exp(steps), shape[axis_at] // shards_of).reshape((-1,) + (1,) * (len(shape) - axis_at - 1))

    level = one(*cuts[0])
    for cut in cuts[1:]:
        level = level * one(*cut)
    return level


def scatter_about(key, extent, scale, bound, shards=(), held_as=jnp.bfloat16):
    level = shard_levels(key, extent, shards, -0.22, 0.18) if shards else 1.0
    entries = jax.random.normal(key, extent, jnp.float32) * scale * level
    return jnp.minimum(jnp.maximum(entries, -bound), bound).astype(held_as)


def setup_inputs(seed: int = 0) -> dict:
    splits = jax.random.split(jax.random.key(seed), 9)
    return {
        "sub_field": scatter_about(splits[0], (NSUB * SC, R), 0.4, 2.4, ((0, 32),), jnp.float32),
        "reluctivity": jnp.clip(jnp.exp(math.log(3.0) - 2.3025851 * jax.random.uniform(splits[1], (2, NSUB * SC, R), jnp.float32) ** shard_levels(splits[1], (2, NSUB * SC, R), ((1, 32),), -0.2, 0.2)), 0.3, 3.0),
        "stride": plant(jax.random.randint(splits[2], (NSUB,), 2, SC // 4), jax.random.fold_in(splits[2], 1), 2, (SC // 4) - 1).astype(jnp.int32),
        "counts": draw_counts(jax.random.fold_in(splits[8], 71), 0),
        "source_cell": plant(jax.random.randint(splits[4], (NSUB, N_ROW, CAP), 0, SC), jax.random.fold_in(splits[4], 1), 0, SC - 1).astype(jnp.int32),
        "target_row": plant(jax.random.randint(splits[5], (N_ROW, N_COL, N_ROW, CAP), 0, WIN * TB), jax.random.fold_in(splits[5], 1), 0, (WIN * TB) - 1).astype(jnp.int32),
        "lower_tiles": scatter_about(splits[6], (PAIRS, NB, NB), (NB * WIN) ** -0.5, 0.046875, ((1, 8), (2, 4)), jnp.float32),
        "diag_inverse": draw_diag_inverse(jax.random.fold_in(splits[8], 71), 0),
    }


def sweep_subdomain(field, radial_nu, tangent_nu, stride_value):
    cell_index = jnp.arange(field.shape[0], dtype=jnp.int32)[:, None]
    radial_prev = jnp.where(cell_index >= stride_value, jnp.roll(field, stride_value, axis=0), 0.0)
    tangent_prev = jnp.where(cell_index >= 1, jnp.roll(field, 1, axis=0), 0.0)
    return radial_nu * (field - radial_prev) + tangent_nu * (field - tangent_prev)


def exact_dot(left, right):
    return jnp.dot(left, right, precision=lax.Precision.HIGHEST, preferred_element_type=jnp.float32)


def reference(sub_field, reluctivity, stride, counts, source_cell, target_row, lower_tiles, diag_inverse):
    subdomains = N_ROW * N_COL
    fields = sub_field.reshape(subdomains, SC, R)
    coefficients = reluctivity.reshape(2, subdomains, SC, R)
    swept = jax.vmap(sweep_subdomain)(fields, coefficients[0], coefficients[1], stride)
    owners = jnp.arange(subdomains, dtype=jnp.int32)[:, None, None]
    picked = swept[owners, source_cell]
    live = jnp.arange(CAP, dtype=jnp.int32)[None, None, :] < counts[:, :, None]
    picked = jnp.where(live[:, :, :, None], picked, 0.0)
    targets = jnp.transpose(target_row, (2, 1, 0, 3)).reshape(subdomains, N_ROW, CAP)
    grid_index = jnp.arange(N_ROW, dtype=jnp.int32)[None, :, None]
    global_row = (targets // TB) * NB + grid_index * TB + targets % TB
    rhs = jnp.zeros((WIN * NB, R), jnp.float32).at[global_row.reshape(-1)].add(picked.reshape(-1, R))
    rhs = rhs.reshape(WIN, NB, R)
    solved = []
    for row_block in range(WIN):
        residual = rhs[row_block]
        for earlier in range(row_block):
            residual = residual - exact_dot(lower_tiles[row_block * (row_block - 1) // 2 + earlier], solved[earlier])
        solved.append(exact_dot(diag_inverse[row_block], residual))
    return jnp.stack(solved).reshape(WIN, N_COL, CB, R)
```

```python
import functools

import jax
import jax.numpy as jnp
from jax import lax
from jax.experimental import pallas as pl
from jax.experimental.pallas import tpu as pltpu
from jax.sharding import PartitionSpec as P

MESH = pl.DeviceIdType.MESH
CORES = 2
PICKS = 8
CHUNKS = 4
DEPTH = 4
PARTS = 2


def pair_index(later_block, earlier_block):
    return later_block * (later_block - 1) // 2 + earlier_block


def halves(value, axis):
    high = value.astype(jnp.bfloat16)
    low = (value - high.astype(jnp.float32)).astype(jnp.bfloat16)
    return jnp.concatenate([high, low], axis=axis)


def split_product(left, right_halves):
    rows, rotor = left.shape[0], right_halves.shape[1] // 2
    full = jnp.dot(halves(left, 0), right_halves, preferred_element_type=jnp.float32)
    return (full[rows:, rotor:] + full[rows:, :rotor] + full[:rows, rotor:]) + full[:rows, :rotor]


def swap_lanes(value):
    return pltpu.roll(value, value.shape[1] // 2, 1)


def solve_kernel(
    n_row, n_col, stride, counts_hbm, source_hbm, target_hbm, field_hbm, nu_hbm, lower_hbm,
    diag_hbm, out_ref, counts, source, target_rows, field, nu, picked, packs, received, arrived,
    lower, diag, acc, px, x_in, eb, part, rs_in, ysh, yb, fin_in, own, theirs,
    f_sem, t_sems, p_sems, w_sem, d_sem, wr_sems, dr_sems, x_sems, rs_send, rs_recv, ag_send, ag_recv, fin_send,
    fin_recv, o_sems,
):
    blocks, _, share, tile_rows = diag.shape
    rotor = px.shape[1]
    n_x = n_col // CORES
    n_y = n_row // DEPTH
    first_owner, n_own = n_y, n_row // 2
    strip = part.shape[1]
    per_piece = part.shape[0] // n_row
    r = lax.axis_index("row")
    c = lax.axis_index("col")
    core = lax.rem(c, CORES)
    other = 1 - core
    c_other = c + 1 - 2 * core
    core_peer = {"col": c_other}
    x_peer = [{"col": lax.rem(c + CORES * s, n_col)} for s in range(1, n_x)]
    row_at = [lax.rem(r + s, n_row) for s in range(n_row)]
    cols_at = [c, c_other]
    peers = [core_peer] + x_peer
    peers += [{"row": g, "col": k} for g in row_at[1:] for k in cols_at]
    slots = source.shape[2]
    half_slots = slots // 2
    half_k = share // PARTS
    is_owner = jnp.logical_and(r >= first_owner, r < first_owner + n_own)
    me_owner = jnp.clip(r - first_owner, 0, n_own - 1)
    owner_at = [lax.rem(r + t, n_own) for t in range(n_own)]
    owner_away = [first_owner + o != r for o in owner_at]

    def first_half(shape):
        return lax.broadcasted_iota(jnp.int32, shape, 1) < rotor // 2

    def merge(left, right):
        return jnp.where(first_half(left.shape), left, right)

    def between(src, dst, send, recv, device):
        return pltpu.make_async_remote_copy(
            src_ref=src, dst_ref=dst, send_sem=send, recv_sem=recv,
            device_id=device, device_id_type=MESH,
        )

    def describe(src, dst, sems, at, device):
        return between(src, dst, sems.at[(0,) + at], sems.at[(1,) + at], device)

    def remote(src, dst, sems, at, device):
        copy = describe(src, dst, sems, at, device)
        copy.start()
        return copy

    def load_lower(k):
        return pltpu.make_async_copy(lower_hbm.at[k], lower.at[k, core], w_sem.at[k])

    def share_lower(k):
        return describe(lower_hbm.at[k], lower.at[k, core], wr_sems, (k,), core_peer)

    def load_diag(k):
        return pltpu.make_async_copy(diag_hbm.at[k], diag.at[k, core], d_sem.at[k])

    def share_diag(k):
        return describe(diag_hbm.at[k], diag.at[k, core], dr_sems, (k,), core_peer)

    def finish(copies):
        for copy in copies:
            copy.wait()

    loads = (
        pltpu.make_async_copy(counts_hbm, counts, f_sem.at[3]),
        pltpu.make_async_copy(source_hbm, source, f_sem.at[4]),
        pltpu.make_async_copy(target_hbm.at[0, 0], target_rows.at[core], f_sem.at[2]),
        pltpu.make_async_copy(field_hbm, field, f_sem.at[0]),
        pltpu.make_async_copy(nu_hbm, nu, f_sem.at[1]),
    )
    for copy in loads:
        copy.start()
    barrier = pltpu.get_barrier_semaphore()
    for p in peers:
        pl.semaphore_signal(barrier, inc=1, device_id=p, device_id_type=MESH)

    def pick(s):
        g = row_at[s]
        band = stride[0]
        live_slots = counts[0, g]

        def group(k8, carry):
            for u in range(PICKS):
                k = k8 * PICKS + u
                m = source[0, g, k]
                here = field[pl.ds(m, 1), :]
                radial = field[pl.ds(jnp.maximum(m - band, 0), 1), :]
                tangent = field[pl.ds(jnp.maximum(m - 1, 0), 1), :]
                has_radial = jnp.where(m >= band, 1.0, 0.0)
                has_tangent = jnp.where(m >= 1, 1.0, 0.0)
                live = jnp.where(k < live_slots, 1.0, 0.0)
                swept = nu[0, pl.ds(m, 1), :] * (here - radial * has_radial) + nu[
                    1, pl.ds(m, 1), :
                ] * (here - tangent * has_tangent)
                picked[s, pl.ds(k, 1), :] = swept * live
            return carry

        lax.fori_loop(0, slots // PICKS, group, 0)
        early, late = picked[s, :half_slots], picked[s, half_slots:]
        packs[s, 0] = merge(early, swap_lanes(late))
        packs[s, 1] = merge(swap_lanes(early), late)

    for copy in loads:
        copy.wait()
    mine = r * CORES + core
    order = [("d", 0)]
    for j in range(blocks - 1):
        order += [("l", pair_index(j + 1, j)), ("d", j + 1)]
        order += [("l", pair_index(i, j)) for i in range(j + 2, blocks)]
    for kind, k in order:
        (load_diag(k) if kind == "d" else load_lower(k)).start()
    sent = []
    for s in list(range(1, n_row)) + [0]:
        pick(s)
        if s == 1:
            pl.semaphore_wait(barrier, len(peers))
            sent.append(
                remote(target_rows.at[core], target_rows.at[core], t_sems, (0,), core_peer)
            )
        for w, (k, col) in enumerate(((core, c), (other, c_other))):
            if s or w:
                sent.append(remote(
                    packs.at[s, k], received.at[mine], p_sems, (s, w), {"row": row_at[s], "col": col},
                ))
    for kind, k in order:
        (share_diag(k) if kind == "d" else share_lower(k)).start()
    received[mine] = packs[0, core]
    finish(sent)
    arrived[...] = halves(received[...].reshape(arrived.shape[0], rotor), 1)

    targets = [
        jnp.concatenate(
            [
                target_rows[k, q:q + 1, h * half_slots:(h + 1) * half_slots]
                for q in range(n_row) for k in range(CORES)
            ],
            axis=1,
        )
        for h in range(2)
    ]

    def place(i):
        here = lax.broadcasted_iota(jnp.int32, (tile_rows, arrived.shape[0]), 0) + i * tile_rows
        sums = []
        for h in range(2):
            chosen = jnp.where(here == targets[h], 1.0, 0.0).astype(jnp.bfloat16)
            full = jnp.dot(chosen, arrived[...], preferred_element_type=jnp.float32)
            sums.append(full[:, :rotor] + full[:, rotor:])
        acc[i] = merge(*sums)

    place(0)

    def lower_part(i, j, h):
        at = pl.ds(h * half_k, half_k)
        left = lower[pair_index(i, j), :, :, at].reshape(CORES * tile_rows, half_k)
        product = split_product(left, yb[at])
        acc[i] = acc[i] - merge(product[:tile_rows], product[tile_rows:])

    def lower_step(i, j):
        k = pair_index(i, j)
        finish([load_lower(k), share_lower(k)])
        for h in range(PARTS):
            lower_part(i, j, h)

    def reduce_copy(q, t):
        o = owner_at[t]
        return between(
            part.at[q * n_own + o], rs_in.at[r, q], rs_send.at[q, t], rs_recv.at[r, q],
            {"row": first_owner + o},
        )

    def reduce_arrival(q, s):
        src = row_at[s]
        return between(
            part.at[q], rs_in.at[src, q], rs_send.at[q, 0], rs_recv.at[src, q], {"row": src}
        )

    def gather_copy(q, s):
        at = q * n_own + me_owner
        return between(
            ysh.at[at], ysh.at[at], ag_send.at[q, s - 1], ag_recv.at[at], {"row": row_at[s]}
        )

    def gather_arrival(q, t):
        at = q * n_own + owner_at[t]
        return between(
            ysh.at[at], ysh.at[at], ag_send.at[q, 0], ag_recv.at[at],
            {"row": first_owner + owner_at[t]},
        )

    def piece_of(g):
        return pl.ds(g * per_piece, per_piece)

    def final_copy(g):
        return between(
            part.at[piece_of(g)], fin_in.at[r], fin_send.at[g], fin_recv.at[r], {"row": g}
        )

    def final_arrival(s):
        src = row_at[s]
        return between(
            part.at[piece_of(0)], fin_in.at[src], fin_send.at[0], fin_recv.at[src], {"row": src}
        )

    def own_copy(first, count, at):
        span = pl.ds(first, count)
        return describe(own.at[span], theirs.at[span], o_sems, (at,), core_peer)

    def write_out(i):
        swapped = swap_lanes(theirs[i])
        low, high = merge(own[i], swapped), merge(swapped, own[i])
        out_ref[i] = jnp.where(core == 0, low, high)

    def step(i, carry):
        parity = lax.rem(i, 2)

        def deferred(*turns):
            for t in turns:
                @pl.when(jnp.logical_and(i > 0, i + 1 + t < blocks))
                def _():
                    lower_step(i + 1 + t, i - 1)

            @pl.when(i == 0)
            def _():
                for t in turns:
                    if 1 + t < blocks:
                        place(1 + t)

        top, bottom = acc[i, :tile_rows // 2], acc[i, tile_rows // 2:]
        px[...] = merge(top, bottom) + swap_lanes(merge(bottom, top))
        across = [
            remote(px, x_in.at[parity, s], x_sems, (parity, s), p) for s, p in enumerate(x_peer)
        ]
        deferred(0, 1)
        finish([load_diag(i), share_diag(i)])
        finish(across)
        total = px[...]
        for s in range(n_x - 1):
            total = total + x_in[parity, s]
        swapped = swap_lanes(total)
        eb[...] = halves(
            jnp.concatenate([merge(total, swapped), merge(swapped, total)], axis=0), 1
        )

        def diag_chunk(q):
            rows = share // CHUNKS
            left = diag[i, :, q * rows:(q + 1) * rows].reshape(CORES * rows, tile_rows)
            product = split_product(left, eb[...])
            value = merge(product[:rows], product[rows:])
            part[q * n_own:(q + 1) * n_own] = value.reshape(n_own, strip, rotor)

        @pl.when(i < blocks - 1)
        def _():
            for q in range(CHUNKS):
                diag_chunk(q)
                for t in range(n_own):
                    @pl.when(owner_away[t])
                    def _():
                        reduce_copy(q, t).start()
            deferred(2, 3)

            @pl.when(is_owner)
            def _():
                for q in range(CHUNKS):
                    at = q * n_own + me_owner
                    total = part[at]
                    for s in range(1, n_row):
                        reduce_arrival(q, s).wait_recv()
                    for s in range(1, n_row):
                        total = total + rs_in[row_at[s], q]
                    ysh[at] = total
                    for s in range(1, n_row):
                        gather_copy(q, s).start()

            deferred(*range(4, blocks - 1))
            for h in range(PARTS):
                per_part = CHUNKS // PARTS
                for q in range(h * per_part, (h + 1) * per_part):
                    for t in range(n_own):
                        @pl.when(owner_away[t])
                        def _():
                            gather_arrival(q, t).wait_recv()
                strips = per_part * n_own
                value = ysh[h * strips:(h + 1) * strips].reshape(half_k, rotor)
                yb[h * half_k:(h + 1) * half_k] = halves(value, 1)
                if h == 0:
                    k = pair_index(i + 1, i)
                    finish([load_lower(k), share_lower(k)])
                lower_part(i + 1, i, h)
            own[i] = ysh[piece_of(r)].reshape(own.shape[1:])
            for q in range(CHUNKS):
                for t in range(n_own):
                    @pl.when(owner_away[t])
                    def _():
                        reduce_copy(q, t).wait_send()

            @pl.when(is_owner)
            def _():
                for q in range(CHUNKS):
                    for s in range(1, n_row):
                        gather_copy(q, s).wait_send()

        @pl.when(i == blocks - 1)
        def _():
            earlier = own_copy(0, blocks - 1, 0)
            earlier.start()
            for q in range(CHUNKS):
                diag_chunk(q)
                for g in range(q * n_row // CHUNKS, (q + 1) * n_row // CHUNKS):
                    @pl.when(g != r)
                    def _():
                        final_copy(g).start()
            earlier.wait()
            for j in range(blocks - 1):
                write_out(j)
            total = part[piece_of(r)]
            for s in range(1, n_row):
                final_arrival(s).wait_recv()
                total = total + fin_in[row_at[s]]
            own[blocks - 1] = total.reshape(own.shape[1:])
            latest = own_copy(blocks - 1, 1, 1)
            latest.start()
            latest.wait()
            write_out(blocks - 1)
            for g in range(n_row):
                @pl.when(g != r)
                def _():
                    final_copy(g).wait_send()

        return carry

    lax.fori_loop(0, blocks, step, 0)


def per_device(
    sub_field, reluctivity, stride, counts, source_cell, target_row, lower_tiles, diag_inverse
):
    n_row, n_col = lax.axis_size("row"), lax.axis_size("col")
    blocks, tile_rows, rotor = diag_inverse.shape[0], lower_tiles.shape[1], sub_field.shape[1]
    cap = source_cell.shape[2]
    pairs = lower_tiles.shape[0]
    share = diag_inverse.shape[1]
    piece = share // n_row
    n_x = n_col // CORES
    n_own = n_row // 2
    strips = CHUNKS * n_own
    strip = share // strips
    f32 = jnp.float32
    bf16 = jnp.bfloat16
    vmem = pl.BlockSpec(memory_space=pltpu.VMEM)
    hbm = pl.BlockSpec(memory_space=pltpu.HBM)
    dma = pltpu.SemaphoreType.DMA
    pieces = pl.pallas_call(
        functools.partial(solve_kernel, n_row, n_col),
        out_shape=jax.ShapeDtypeStruct((blocks, piece, rotor), f32),
        in_specs=[pl.BlockSpec(memory_space=pltpu.SMEM)] + [hbm] * 7,
        out_specs=vmem,
        scratch_shapes=[
            pltpu.SMEM(counts.shape, jnp.int32),
            pltpu.SMEM(source_cell.shape, jnp.int32),
            pltpu.VMEM((CORES, n_row, cap), jnp.int32),
            pltpu.VMEM(sub_field.shape, f32),
            pltpu.VMEM(reluctivity.shape, f32),
            pltpu.VMEM((n_row, cap, rotor), f32),
            pltpu.VMEM((n_row, CORES, cap // 2, rotor), f32),
            pltpu.VMEM((n_row * CORES, cap // 2, rotor), f32),
            pltpu.VMEM((n_row * cap, 2 * rotor), bf16),
            pltpu.VMEM((pairs, CORES) + lower_tiles.shape[1:], f32),
            pltpu.VMEM((blocks, CORES) + diag_inverse.shape[1:], f32),
            pltpu.VMEM((blocks, tile_rows, rotor), f32),
            pltpu.VMEM((tile_rows // 2, rotor), f32),
            pltpu.VMEM((2, n_x - 1, tile_rows // 2, rotor), f32),
            pltpu.VMEM((tile_rows, 2 * rotor), bf16),
            pltpu.VMEM((strips, strip, rotor), f32),
            pltpu.VMEM((n_row, CHUNKS, strip, rotor), f32),
            pltpu.VMEM((strips, strip, rotor), f32),
            pltpu.VMEM((share, 2 * rotor), bf16),
            pltpu.VMEM((n_row, strips // n_row, strip, rotor), f32),
            pltpu.VMEM((blocks, piece, rotor), f32),
            pltpu.VMEM((blocks, piece, rotor), f32),
            dma((5,)),
            dma((2, 1)),
            dma((2, n_row, CORES)),
            dma((pairs,)),
            dma((blocks,)),
            dma((2, pairs)),
            dma((2, blocks)),
            dma((2, 2, n_x - 1)),
            dma((CHUNKS, n_own)),
            dma((n_row, CHUNKS)),
            dma((CHUNKS, n_row - 1)),
            dma((strips,)),
            dma((n_row,)),
            dma((n_row,)),
            dma((2, 2)),
        ],
        compiler_params=pltpu.CompilerParams(
            collective_id=0, has_side_effects=True, vmem_limit_bytes=67043328
        ),
    )(
        stride, counts, source_cell, target_row, sub_field, reluctivity, lower_tiles, diag_inverse
    )
    return pieces[:, None]


def solution(mesh):
    placed = (
        P(("row", "col"), None),
        P(None, ("row", "col"), None),
        P(("row", "col")),
        P(("row", "col"), None),
        P(("row", "col"), None, None),
        P("row", "col", None, None),
        P(None, "row", "col"),
        P(None, "col", "row"),
    )
    return jax.shard_map(
        per_device,
        mesh=mesh,
        in_specs=placed,
        out_specs=P(None, "col", "row", None),
        check_vma=False,
    )
```

```python
import functools

import jax
import jax.numpy as jnp
from jax import lax
from jax.experimental import pallas as pl
from jax.experimental.pallas import tpu as pltpu
from jax.sharding import PartitionSpec as P

MESH = pl.DeviceIdType.MESH
CORES = 2
PICKS = 8
CHAINS = 2
GROUPS = 4
CHUNKS = 1
DEPTH = 4
TURNS = (1, 3)


def pair_index(later_block, earlier_block):
    return later_block * (later_block - 1) // 2 + earlier_block


def halves(value, axis):
    high = value.astype(jnp.bfloat16)
    low = (value - high.astype(jnp.float32)).astype(jnp.bfloat16)
    return jnp.concatenate([high, low], axis=axis)


def product(left_halves, right_halves):
    rotor = right_halves.shape[1] // 2
    right = jnp.concatenate([right_halves, right_halves], axis=0)
    full = jnp.dot(left_halves, right, preferred_element_type=jnp.float32)
    return full[:, :rotor] + full[:, rotor:]


def wide_product(left, right_high, right_low):
    both = halves(left, 1)
    width = left.shape[1]
    left3 = jnp.concatenate([both[:, :width], both], axis=1)
    right3 = jnp.concatenate([right_low, right_high, right_high], axis=0)
    return jnp.dot(left3, right3, preferred_element_type=jnp.float32)


def turn(value, groups):
    width = value.shape[1] // GROUPS
    return pltpu.roll(value, groups % GROUPS * width, 1) if groups % GROUPS else value


def group_of(shape):
    return lax.broadcasted_iota(jnp.int32, shape, 1) // (shape[1] // GROUPS)


def by_group(values):
    group = group_of(values[0].shape)
    low = jnp.where(group == 0, values[0], values[1])
    high = jnp.where(group == 2, values[2], values[3])
    return jnp.where(group < 2, low, high)


def swap_lanes(value):
    return turn(value, GROUPS // 2)


def solve_kernel(
    n_row, n_col, stride, counts_hbm, source_hbm, target_hbm, field_hbm, nu_hbm, lower_hbm,
    diag_hbm, out_ref, counts, source, target_rows, field, nu, picked, packs, received, arrived,
    lower, diag, lb, db, acc, px, x_in, eb, part, rs_in, ysh, yb, last, fin_in, own, theirs,
    f_sem, t_sems, p_sems, w_sem, d_sem, wr_sems, dr_sems, x_sems, rs_send, rs_recv, ag_send, ag_recv, fin_send,
    fin_recv, o_sems,
):
    blocks, _, share, tile_rows = diag.shape
    rotor = px.shape[2]
    n_x = n_col // CORES
    n_y = n_row // DEPTH
    first_owner, n_own = n_y, n_row // 2
    strip = part.shape[1]
    strips = part.shape[0] // CHAINS
    per_piece = 2 * strips // n_row
    r = lax.axis_index("row")
    c = lax.axis_index("col")
    core = lax.rem(c, CORES)
    other = 1 - core
    c_other = c + 1 - 2 * core
    core_peer = {"col": c_other}
    x_peer = [{"col": lax.rem(c + CORES * s, n_col)} for s in range(1, n_x)]
    row_at = [lax.rem(r + s, n_row) for s in range(n_row)]
    cols_at = [c, c_other]
    peers = [core_peer] + x_peer
    peers += [{"row": g, "col": k} for g in row_at[1:] for k in cols_at]
    slots = source.shape[2]
    half_slots = slots // 2
    half_share = share // 2
    quarter = tile_rows // GROUPS
    is_owner = jnp.logical_and(r >= first_owner, r < first_owner + n_own)
    me_owner = jnp.clip(r - first_owner, 0, n_own - 1)
    owner_at = [lax.rem(r + t, n_own) for t in range(n_own)]
    owner_away = [first_owner + o != r for o in owner_at]

    def first_half(shape):
        return lax.broadcasted_iota(jnp.int32, shape, 1) < rotor // 2

    def merge(left, right):
        return jnp.where(first_half(left.shape), left, right)

    def between(src, dst, send, recv, device):
        return pltpu.make_async_remote_copy(
            src_ref=src, dst_ref=dst, send_sem=send, recv_sem=recv,
            device_id=device, device_id_type=MESH,
        )

    def describe(src, dst, sems, at, device):
        return between(src, dst, sems.at[(0,) + at], sems.at[(1,) + at], device)

    def remote(src, dst, sems, at, device):
        copy = describe(src, dst, sems, at, device)
        copy.start()
        return copy

    def load_lower(k):
        return pltpu.make_async_copy(lower_hbm.at[k], lower.at[k, core], w_sem.at[k])

    def share_lower(k):
        return describe(lower_hbm.at[k], lower.at[k, core], wr_sems, (k,), core_peer)

    def load_diag(k):
        return pltpu.make_async_copy(diag_hbm.at[k], diag.at[k, core], d_sem.at[k])

    def share_diag(k):
        return describe(diag_hbm.at[k], diag.at[k, core], dr_sems, (k,), core_peer)

    def finish(copies):
        for copy in copies:
            copy.wait()

    loads = (
        pltpu.make_async_copy(counts_hbm, counts, f_sem.at[3]),
        pltpu.make_async_copy(source_hbm, source, f_sem.at[4]),
        pltpu.make_async_copy(target_hbm.at[0, 0], target_rows.at[core], f_sem.at[2]),
        pltpu.make_async_copy(field_hbm, field, f_sem.at[0]),
        pltpu.make_async_copy(nu_hbm, nu, f_sem.at[1]),
    )
    for copy in loads:
        copy.start()
    barrier = pltpu.get_barrier_semaphore()
    for p in peers:
        pl.semaphore_signal(barrier, inc=1, device_id=p, device_id_type=MESH)

    def pick(s):
        g = row_at[s]
        band = stride[0]
        live_slots = counts[0, g]

        def group(k8, carry):
            for u in range(PICKS):
                k = k8 * PICKS + u
                m = source[0, g, k]
                here = field[pl.ds(m, 1), :]
                radial = field[pl.ds(jnp.maximum(m - band, 0), 1), :]
                tangent = field[pl.ds(jnp.maximum(m - 1, 0), 1), :]
                has_radial = jnp.where(m >= band, 1.0, 0.0)
                has_tangent = jnp.where(m >= 1, 1.0, 0.0)
                live = jnp.where(k < live_slots, 1.0, 0.0)
                swept = nu[0, pl.ds(m, 1), :] * (here - radial * has_radial) + nu[
                    1, pl.ds(m, 1), :
                ] * (here - tangent * has_tangent)
                picked[s, pl.ds(k, 1), :] = swept * live
            return carry

        lax.fori_loop(0, slots // PICKS, group, 0)
        early, late = picked[s, :half_slots], picked[s, half_slots:]
        packs[s, 0] = merge(early, swap_lanes(late))
        packs[s, 1] = merge(swap_lanes(early), late)

    for copy in loads:
        copy.wait()
    mine = r * CORES + core
    order = [("d", 0)]
    for j in range(blocks - 1):
        order += [("l", pair_index(j + 1, j)), ("d", j + 1)]
        order += [("l", pair_index(i, j)) for i in range(j + 2, blocks)]
    for kind, k in order:
        (load_diag(k) if kind == "d" else load_lower(k)).start()
    sent = []
    for s in range(n_row):
        pick(s)
    pl.semaphore_wait(barrier, len(peers))
    for s in list(range(1, n_row)) + [0]:
        for w, (k, col) in enumerate(((core, c), (other, c_other))):
            if s or w:
                sent.append(remote(
                    packs.at[s, k], received.at[mine], p_sems, (s, w), {"row": row_at[s], "col": col},
                ))
    sent.append(remote(target_rows.at[core], target_rows.at[core], t_sems, (0,), core_peer))
    for kind, k in order:
        (share_diag(k) if kind == "d" else share_lower(k)).start()
    received[mine] = packs[0, core]
    finish(sent)
    arrived[...] = halves(received[...].reshape(arrived.shape[0], rotor), 1)

    targets = [
        jnp.concatenate(
            [
                target_rows[k, q:q + 1, h * half_slots:(h + 1) * half_slots]
                for q in range(n_row) for k in range(CORES)
            ],
            axis=1,
        )
        for h in range(2)
    ]

    def place(i):
        here = lax.broadcasted_iota(jnp.int32, (tile_rows, arrived.shape[0]), 0) + i * tile_rows
        sums = []
        for h in range(2):
            chosen = jnp.where(here == targets[h], 1.0, 0.0).astype(jnp.bfloat16)
            full = jnp.dot(chosen, arrived[...], preferred_element_type=jnp.float32)
            sums.append(full[:, :rotor] + full[:, rotor:])
        value = merge(*sums)
        even = lax.rem(group_of(value.shape), 2) == 0
        acc[i, 0] = jnp.where(even, value, 0.0)
        acc[i, 1] = jnp.where(even, 0.0, value)

    place(0)

    def lower_half(k, h):
        return lower[k, :, :, h * half_share:(h + 1) * half_share].reshape(
            CORES * tile_rows, half_share
        )

    def subtract(i, a, products, at):
        acc[i, a] = acc[i, a] - by_group([
            products[h][v * tile_rows:(v + 1) * tile_rows, at]
            for v in range(CORES) for h in range(2)
        ])

    def lower_step(i, j):
        k = pair_index(i, j)
        finish([load_lower(k), share_lower(k)])
        high = jnp.concatenate([yb[a, :, :rotor] for a in range(CHAINS)], axis=1)
        low = jnp.concatenate([yb[a, :, rotor:] for a in range(CHAINS)], axis=1)
        products = [wide_product(lower_half(k, h), high, low) for h in range(2)]
        for a in range(CHAINS):
            subtract(i, a, products, slice(a * rotor, (a + 1) * rotor))

    def prepare_lower(k):
        finish([load_lower(k), share_lower(k)])
        for h in range(2):
            lb[h] = halves(lower_half(k, h), 1)

    def prepare_diag(i):
        finish([load_diag(i), share_diag(i)])
        rows = half_share // CHUNKS
        for q in range(CHUNKS):
            for h in range(2):
                at = h * half_share + q * rows
                db[q, h * CORES * rows:(h + 1) * CORES * rows] = halves(
                    diag[i, :, at:at + rows].reshape(CORES * rows, tile_rows), 1
                )

    def across_copies(i, a):
        parity = lax.rem(i, 2)
        return [
            describe(px.at[a], x_in.at[parity, a, s], x_sems, (parity, a, s), p)
            for s, p in enumerate(x_peer)
        ]

    def send_across(i, a):
        rows = [acc[i, a, b * quarter:(b + 1) * quarter] for b in range(GROUPS)]
        px[a] = sum(
            turn(by_group([rows[(g - d) % GROUPS] for g in range(GROUPS)]), -d)
            for d in range(GROUPS)
        )
        for copy in across_copies(i, a):
            copy.start()

    def reduce_copy(q, t):
        o = owner_at[t]
        return between(
            part.at[q * n_own + o], rs_in.at[r, q], rs_send.at[q, t], rs_recv.at[r, q],
            {"row": first_owner + o},
        )

    def reduce_arrival(q, s):
        src = row_at[s]
        return between(
            part.at[q], rs_in.at[src, q], rs_send.at[q, 0], rs_recv.at[src, q], {"row": src}
        )

    def gather_copy(q, s):
        at = q * n_own + me_owner
        return between(
            ysh.at[at], ysh.at[at], ag_send.at[q, s - 1], ag_recv.at[at], {"row": row_at[s]}
        )

    def gather_arrival(q, t):
        at = q * n_own + owner_at[t]
        return between(
            ysh.at[at], ysh.at[at], ag_send.at[q, 0], ag_recv.at[at],
            {"row": first_owner + owner_at[t]},
        )

    def arranged(first, second, half):
        even = lax.rem(group_of(first.shape), 2) == 0
        early = jnp.where(even, first, turn(second, 1))
        late = jnp.where(even, turn(first, -1), second)
        return jnp.where(half == 0, early, late)

    def final_copy(g):
        return between(
            last.at[g], fin_in.at[r], fin_send.at[g], fin_recv.at[r], {"row": g}
        )

    def final_arrival(s):
        src = row_at[s]
        return between(
            last.at[0], fin_in.at[src], fin_send.at[0], fin_recv.at[src], {"row": src}
        )

    def own_copy(first, count, at):
        span = pl.ds(first, count)
        return describe(own.at[span], theirs.at[span], o_sems, (at,), core_peer)

    def write_out(i):
        swapped = swap_lanes(theirs[i])
        low, high = merge(own[i], swapped), merge(swapped, own[i])
        out_ref[i] = jnp.where(core == 0, low, high)

    def step(i, carry):
        parity = lax.rem(i, 2)

        def deferred(*turns):
            for t in turns:
                @pl.when(jnp.logical_and(i > 0, i + 1 + t < blocks))
                def _():
                    lower_step(i + 1 + t, i - 1)

            @pl.when(i == 0)
            def _():
                for t in turns:
                    if 1 + t < blocks:
                        place(1 + t)

        prepare_diag(i)
        deferred(*range(0, TURNS[0]))

        def residual(a):
            finish(across_copies(i, a))
            total = px[a]
            for s in range(n_x - 1):
                total = total + x_in[parity, a, s]
            turned = [turn(total, d) for d in range(GROUPS)]
            spread = [
                by_group([turned[(g - b) % GROUPS] for g in range(GROUPS)])
                for b in range(GROUPS)
            ]
            eb[a] = halves(jnp.concatenate(spread, axis=0), 1)

        def diag_chunk(a, q):
            rows = half_share // CHUNKS
            value = product(db[q], eb[a])
            value = by_group([
                value[(h * CORES + v) * rows:(h * CORES + v + 1) * rows]
                for v in range(CORES) for h in range(2)
            ])
            at = (a * CHUNKS + q) * n_own
            part[at:at + n_own] = value.reshape(n_own, strip, rotor)

        @pl.when(i < blocks - 1)
        def _():
            for a in range(CHAINS):
                residual(a)
                for q in range(CHUNKS):
                    diag_chunk(a, q)
                    for t in range(n_own):
                        @pl.when(owner_away[t])
                        def _():
                            reduce_copy(a * CHUNKS + q, t).start()
            prepare_lower(pair_index(i + 1, i))
            deferred(*range(TURNS[0], TURNS[1]))

            @pl.when(is_owner)
            def _():
                for q in range(CHAINS * CHUNKS):
                    at = q * n_own + me_owner
                    total = part[at]
                    for s in range(1, n_row):
                        reduce_arrival(q, s).wait_recv()
                    for s in range(1, n_row):
                        total = total + rs_in[row_at[s], q]
                    ysh[at] = total
                    for s in range(1, n_row):
                        gather_copy(q, s).start()

            deferred(*range(TURNS[1], blocks - 1))
            for a in range(CHAINS):
                for q in range(a * CHUNKS, (a + 1) * CHUNKS):
                    for t in range(n_own):
                        @pl.when(owner_away[t])
                        def _():
                            gather_arrival(q, t).wait_recv()
                value = ysh[a * strips:(a + 1) * strips].reshape(half_share, rotor)
                yb[a] = halves(value, 1)
                subtract(i + 1, a, [product(lb[h], yb[a]) for h in range(2)], slice(rotor))
                send_across(i + 1, a)
            at = lax.rem(r, n_row // 2) * per_piece
            first, second = (
                ysh[pl.ds(a * strips + at, per_piece)].reshape(own.shape[1:])
                for a in range(CHAINS)
            )
            own[i] = arranged(first, second, lax.div(r, n_row // 2))
            for q in range(CHAINS * CHUNKS):
                for t in range(n_own):
                    @pl.when(owner_away[t])
                    def _():
                        reduce_copy(q, t).wait_send()

            @pl.when(is_owner)
            def _():
                for q in range(CHAINS * CHUNKS):
                    for s in range(1, n_row):
                        gather_copy(q, s).wait_send()

        @pl.when(i == blocks - 1)
        def _():
            earlier = own_copy(0, blocks - 1, 0)
            earlier.start()
            for a in range(CHAINS):
                residual(a)
                for q in range(CHUNKS):
                    diag_chunk(a, q)
            for g in range(n_row):
                at = g % (n_row // 2) * per_piece
                first, second = (
                    part[a * strips + at:a * strips + at + per_piece].reshape(own.shape[1:])
                    for a in range(CHAINS)
                )
                last[g] = arranged(first, second, g // (n_row // 2))

                @pl.when(g != r)
                def _():
                    final_copy(g).start()
            earlier.wait()
            for j in range(blocks - 1):
                write_out(j)
            total = last[r]
            for s in range(1, n_row):
                final_arrival(s).wait_recv()
                total = total + fin_in[row_at[s]]
            own[blocks - 1] = total
            latest = own_copy(blocks - 1, 1, 1)
            latest.start()
            latest.wait()
            write_out(blocks - 1)
            for g in range(n_row):
                @pl.when(g != r)
                def _():
                    final_copy(g).wait_send()

        return carry

    for a in range(CHAINS):
        send_across(0, a)
    lax.fori_loop(0, blocks, step, 0)


def per_device(
    sub_field, reluctivity, stride, counts, source_cell, target_row, lower_tiles, diag_inverse
):
    n_row, n_col = lax.axis_size("row"), lax.axis_size("col")
    blocks, tile_rows, rotor = diag_inverse.shape[0], lower_tiles.shape[1], sub_field.shape[1]
    cap = source_cell.shape[2]
    pairs = lower_tiles.shape[0]
    share = diag_inverse.shape[1]
    piece = share // n_row
    n_x = n_col // CORES
    n_own = n_row // 2
    strips = CHAINS * CHUNKS * n_own
    strip = share // strips
    f32 = jnp.float32
    bf16 = jnp.bfloat16
    vmem = pl.BlockSpec(memory_space=pltpu.VMEM)
    hbm = pl.BlockSpec(memory_space=pltpu.HBM)
    dma = pltpu.SemaphoreType.DMA
    pieces = pl.pallas_call(
        functools.partial(solve_kernel, n_row, n_col),
        out_shape=jax.ShapeDtypeStruct((blocks, piece, rotor), f32),
        in_specs=[pl.BlockSpec(memory_space=pltpu.SMEM)] + [hbm] * 7,
        out_specs=vmem,
        scratch_shapes=[
            pltpu.SMEM(counts.shape, jnp.int32),
            pltpu.SMEM(source_cell.shape, jnp.int32),
            pltpu.VMEM((CORES, n_row, cap), jnp.int32),
            pltpu.VMEM(sub_field.shape, f32),
            pltpu.VMEM(reluctivity.shape, f32),
            pltpu.VMEM((n_row, cap, rotor), f32),
            pltpu.VMEM((n_row, CORES, cap // 2, rotor), f32),
            pltpu.VMEM((n_row * CORES, cap // 2, rotor), f32),
            pltpu.VMEM((n_row * cap, 2 * rotor), bf16),
            pltpu.VMEM((pairs, CORES) + lower_tiles.shape[1:], f32),
            pltpu.VMEM((blocks, CORES) + diag_inverse.shape[1:], f32),
            pltpu.VMEM((2, CORES * tile_rows, share), bf16),
            pltpu.VMEM((CHUNKS, CORES * share // CHUNKS, 2 * tile_rows), bf16),
            pltpu.VMEM((blocks, CHAINS, tile_rows, rotor), f32),
            pltpu.VMEM((CHAINS, tile_rows // GROUPS, rotor), f32),
            pltpu.VMEM((2, CHAINS, n_x - 1, tile_rows // GROUPS, rotor), f32),
            pltpu.VMEM((CHAINS, tile_rows, 2 * rotor), bf16),
            pltpu.VMEM((strips, strip, rotor), f32),
            pltpu.VMEM((n_row, CHAINS * CHUNKS, strip, rotor), f32),
            pltpu.VMEM((strips, strip, rotor), f32),
            pltpu.VMEM((CHAINS, share // 2, 2 * rotor), bf16),
            pltpu.VMEM((n_row, piece, rotor), f32),
            pltpu.VMEM((n_row, piece, rotor), f32),
            pltpu.VMEM((blocks, piece, rotor), f32),
            pltpu.VMEM((blocks, piece, rotor), f32),
            dma((5,)),
            dma((2, 1)),
            dma((2, n_row, CORES)),
            dma((pairs,)),
            dma((blocks,)),
            dma((2, pairs)),
            dma((2, blocks)),
            dma((2, 2, CHAINS, n_x - 1)),
            dma((CHAINS * CHUNKS, n_own)),
            dma((n_row, CHAINS * CHUNKS)),
            dma((CHAINS * CHUNKS, n_row - 1)),
            dma((strips,)),
            dma((n_row,)),
            dma((n_row,)),
            dma((2, 2)),
        ],
        compiler_params=pltpu.CompilerParams(
            collective_id=0, has_side_effects=True, vmem_limit_bytes=67043328
        ),
    )(
        stride, counts, source_cell, target_row, sub_field, reluctivity, lower_tiles, diag_inverse
    )
    return pieces[:, None]


def solution(mesh):
    placed = (
        P(("row", "col"), None),
        P(None, ("row", "col"), None),
        P(("row", "col")),
        P(("row", "col"), None),
        P(("row", "col"), None, None),
        P("row", "col", None, None),
        P(None, "row", "col"),
        P(None, "col", "row"),
    )
    return jax.shard_map(
        per_device,
        mesh=mesh,
        in_specs=placed,
        out_specs=P(None, "col", "row", None),
        check_vma=False,
    )
```

```python
import functools

import jax
import jax.numpy as jnp
from jax import lax
from jax.experimental import pallas as pl
from jax.experimental.pallas import tpu as pltpu
from jax.sharding import PartitionSpec as P

MESH = pl.DeviceIdType.MESH
CORES = 2
PICKS = 8
CHAINS = 2
GROUPS = 2 * CHAINS
CHUNKS = 2
DEPTH = 4
TURNS = 2
NEAR = 4


def pair_index(later_block, earlier_block):
    return later_block * (later_block - 1) // 2 + earlier_block


def halves(value, axis):
    high = value.astype(jnp.bfloat16)
    low = (value - high.astype(jnp.float32)).astype(jnp.bfloat16)
    return jnp.concatenate([high, low], axis=axis)


def product(left_halves, right_halves):
    rotor = right_halves.shape[1] // 2
    right = jnp.concatenate([right_halves, right_halves], axis=0)
    full = jnp.dot(left_halves, right, preferred_element_type=jnp.float32)
    return full[:, :rotor] + full[:, rotor:]


def turn(value, groups):
    width = value.shape[1] // GROUPS
    return pltpu.roll(value, groups % GROUPS * width, 1) if groups % GROUPS else value


def group_of(shape):
    return lax.broadcasted_iota(jnp.int32, shape, 1) // (shape[1] // GROUPS)


def by_group(values):
    group = group_of(values[0].shape)

    def among(first, last):
        if last - first == 1:
            return values[first]
        middle = (first + last) // 2
        return jnp.where(group < middle, among(first, middle), among(middle, last))

    return among(0, len(values))


def arranged(chains, part):
    return by_group([turn(chains[g % CHAINS], g % CHAINS - part) for g in range(GROUPS)])


def swap_lanes(value):
    return turn(value, GROUPS // 2)


def solve_kernel(
    n_row, n_col, stride, counts_hbm, source_hbm, target_hbm, field_hbm, nu_hbm, lower_hbm,
    diag_hbm, out_ref, counts, source, target_rows, field, nu, picked, packs, received, arrived, spot,
    lower, diag, lb, db, acc, px, x_in, eb, part, rs_in, ysh, yb, yd, whole, last, fin_in, own, theirs,
    f_sem, t_sems, p_sems, w_sem, d_sem, wr_sems, dr_sems, x_sems, rs_send, rs_recv, ag_send, ag_recv, fin_send,
    fin_recv, o_sems,
):
    blocks, _, share, tile_rows = diag.shape
    rotor = px.shape[2]
    n_x = n_col // CORES
    n_y = n_row // DEPTH
    first_owner, n_own = n_y, n_row // 2
    strip = part.shape[1]
    strips = part.shape[0] // CHAINS
    piece = share // n_row
    per_piece = piece // strip
    r = lax.axis_index("row")
    c = lax.axis_index("col")
    core = lax.rem(c, CORES)
    other = 1 - core
    c_other = c + 1 - 2 * core
    core_peer = {"col": c_other}
    x_peer = [{"col": lax.rem(c + CORES * s, n_col)} for s in range(1, n_x)]
    row_at = [lax.rem(r + s, n_row) for s in range(n_row)]
    cols_at = [c, c_other]
    peers = [core_peer] + x_peer
    peers += [{"row": g, "col": k} for g in row_at[1:] for k in cols_at]
    slots = source.shape[2]
    half_slots = slots // 2
    span = share // CHAINS
    quarter = tile_rows // GROUPS
    is_owner = jnp.logical_and(r >= first_owner, r < first_owner + n_own)
    me_owner = jnp.clip(r - first_owner, 0, n_own - 1)
    owner_at = [lax.rem(r + t, n_own) for t in range(n_own)]
    owner_away = [first_owner + o != r for o in owner_at]

    def first_half(shape):
        return lax.broadcasted_iota(jnp.int32, shape, 1) < rotor // 2

    def merge(left, right):
        return jnp.where(first_half(left.shape), left, right)

    def between(src, dst, send, recv, device):
        return pltpu.make_async_remote_copy(
            src_ref=src, dst_ref=dst, send_sem=send, recv_sem=recv,
            device_id=device, device_id_type=MESH,
        )

    def describe(src, dst, sems, at, device):
        return between(src, dst, sems.at[(0,) + at], sems.at[(1,) + at], device)

    def remote(src, dst, sems, at, device):
        copy = describe(src, dst, sems, at, device)
        copy.start()
        return copy

    def load_lower(k):
        return pltpu.make_async_copy(lower_hbm.at[k], lower.at[k, core], w_sem.at[k])

    def share_lower(k):
        return describe(lower_hbm.at[k], lower.at[k, core], wr_sems, (k,), core_peer)

    def load_diag(k):
        return pltpu.make_async_copy(diag_hbm.at[k], diag.at[k, core], d_sem.at[k])

    def share_diag(k):
        return describe(diag_hbm.at[k], diag.at[k, core], dr_sems, (k,), core_peer)

    def finish(copies):
        for copy in copies:
            copy.wait()

    loads = (
        pltpu.make_async_copy(counts_hbm, counts, f_sem.at[3]),
        pltpu.make_async_copy(source_hbm, source, f_sem.at[4]),
        pltpu.make_async_copy(target_hbm.at[0, 0], target_rows.at[core], f_sem.at[2]),
        pltpu.make_async_copy(field_hbm, field, f_sem.at[0]),
        pltpu.make_async_copy(nu_hbm, nu, f_sem.at[1]),
    )
    for copy in loads:
        copy.start()
    barrier = pltpu.get_barrier_semaphore()
    for p in peers:
        pl.semaphore_signal(barrier, inc=1, device_id=p, device_id_type=MESH)

    def pick(s):
        g = row_at[s]
        band = stride[0]
        live_slots = counts[0, g]

        def group(k8, carry):
            for u in range(PICKS):
                k = k8 * PICKS + u
                m = source[0, g, k]
                here = field[pl.ds(m, 1), :]
                radial = field[pl.ds(jnp.maximum(m - band, 0), 1), :]
                tangent = field[pl.ds(jnp.maximum(m - 1, 0), 1), :]
                has_radial = jnp.where(m >= band, 1.0, 0.0)
                has_tangent = jnp.where(m >= 1, 1.0, 0.0)
                live = jnp.where(k < live_slots, 1.0, 0.0)
                swept = nu[0, pl.ds(m, 1), :] * (here - radial * has_radial) + nu[
                    1, pl.ds(m, 1), :
                ] * (here - tangent * has_tangent)
                picked[s, pl.ds(k, 1), :] = swept * live
            return carry

        lax.fori_loop(0, slots // PICKS, group, 0)
        early, late = picked[s, :half_slots], picked[s, half_slots:]
        packs[s, 0] = merge(early, swap_lanes(late))
        packs[s, 1] = merge(swap_lanes(early), late)

    for copy in loads:
        copy.wait()
    mine = r * CORES + core
    order = [("d", 0)]
    for j in range(blocks - 1):
        order += [("l", pair_index(j + 1, j)), ("d", j + 1)]
        order += [("l", pair_index(i, j)) for i in range(j + 2, blocks)]
    for kind, k in order:
        (load_diag(k) if kind == "d" else load_lower(k)).start()
    sent = []
    for s in list(range(1, n_row)) + [0]:
        pick(s)
        if s == 1:
            pl.semaphore_wait(barrier, len(peers))
            targets_sent = remote(
                target_rows.at[core], target_rows.at[core], t_sems, (0,), core_peer
            )
        for w, (k, col) in enumerate(((core, c), (other, c_other))):
            if s or w:
                sent.append(remote(
                    packs.at[s, k], received.at[mine], p_sems, (s, w), {"row": row_at[s], "col": col},
                ))
    for kind, k in order:
        (share_diag(k) if kind == "d" else share_lower(k)).start()
    received[mine] = packs[0, core]
    targets_sent.wait()
    targets = [
        jnp.concatenate(
            [
                target_rows[k, q:q + 1, h * half_slots:(h + 1) * half_slots]
                for q in range(n_row) for k in range(CORES)
            ],
            axis=1,
        )
        for h in range(2)
    ]

    def chosen(i, h):
        here = lax.broadcasted_iota(jnp.int32, (tile_rows, arrived.shape[0]), 0) + i * tile_rows
        return jnp.where(here == targets[h], 1.0, 0.0).astype(jnp.bfloat16)

    def place(i, rows=None):
        sums = []
        for h in range(2):
            full = jnp.dot(
                rows[h] if rows else chosen(i, h), arrived[...],
                preferred_element_type=jnp.float32,
            )
            sums.append(full[:, :rotor] + full[:, rotor:])
        acc[i] = merge(*sums)

    for h in range(2):
        spot[h] = chosen(0, h)
    finish(sent)
    arrived[...] = halves(received[...].reshape(arrived.shape[0], rotor), 1)
    place(0, [spot[h] for h in range(2)])

    def lower_half(k, h):
        return lower[k, :, :, h * span:(h + 1) * span].reshape(
            CORES * tile_rows, span
        )

    def lower_step(i, j):
        k = pair_index(i, j)
        finish([load_lower(k), share_lower(k)])
        left = halves(lower[k].reshape(CORES * tile_rows, share), 1)
        value = product(left, yd[j])
        acc[i] = acc[i] - merge(value[:tile_rows], value[tile_rows:])

    def prepare_lower(k):
        finish([load_lower(k), share_lower(k)])
        for h in range(CHAINS):
            lb[h] = halves(lower_half(k, h), 1)

    def prepare_diag(i):
        finish([load_diag(i), share_diag(i)])
        rows = span // CHUNKS
        for q in range(CHUNKS):
            for h in range(CHAINS):
                at = h * span + q * rows
                db[q, h * CORES * rows:(h + 1) * CORES * rows] = halves(
                    diag[i, :, at:at + rows].reshape(CORES * rows, tile_rows), 1
                )

    def across_copies(i, a):
        parity = lax.rem(i, 2)
        return [
            describe(px.at[a], x_in.at[parity, a, s], x_sems, (parity, a, s), p)
            for s, p in enumerate(x_peer)
        ]

    def send_across(i, a, products=None):
        value = acc[i]
        value = jnp.where(lax.rem(group_of(value.shape), CHAINS) == a, value, 0.0)
        if products:
            value = value - by_group([
                products[h][v * tile_rows:(v + 1) * tile_rows]
                for v in range(CORES) for h in range(CHAINS)
            ])
        rows = [value[b * quarter:(b + 1) * quarter] for b in range(GROUPS)]
        px[a] = sum(
            turn(by_group([rows[(g - d) % GROUPS] for g in range(GROUPS)]), -d)
            for d in range(GROUPS)
        )
        for copy in across_copies(i, a):
            copy.start()

    def reduce_copy(q, t):
        o = owner_at[t]
        return between(
            part.at[q * n_own + o], rs_in.at[r, q], rs_send.at[q, t], rs_recv.at[r, q],
            {"row": first_owner + o},
        )

    def reduce_arrival(q, s):
        src = row_at[s]
        return between(
            part.at[q], rs_in.at[src, q], rs_send.at[q, 0], rs_recv.at[src, q], {"row": src}
        )

    def gather_copy(q, s):
        at = q * n_own + me_owner
        return between(
            ysh.at[at], ysh.at[at], ag_send.at[q, s - 1], ag_recv.at[at], {"row": row_at[s]}
        )

    def gather_arrival(q, t):
        at = q * n_own + owner_at[t]
        return between(
            ysh.at[at], ysh.at[at], ag_send.at[q, 0], ag_recv.at[at],
            {"row": first_owner + owner_at[t]},
        )

    def final_copy(g):
        return between(
            last.at[g], fin_in.at[r], fin_send.at[g], fin_recv.at[r], {"row": g}
        )

    def final_arrival(s):
        src = row_at[s]
        return between(
            last.at[0], fin_in.at[src], fin_send.at[0], fin_recv.at[src], {"row": src}
        )

    def own_copy(first, count, at):
        span = pl.ds(first, count)
        return describe(own.at[span], theirs.at[span], o_sems, (at,), core_peer)

    def write_out(i):
        swapped = swap_lanes(theirs[i])
        low, high = merge(own[i], swapped), merge(swapped, own[i])
        out_ref[i] = jnp.where(core == 0, low, high)

    def step(i, carry):
        parity = lax.rem(i, 2)

        def deferred(*turns):
            for t in turns:
                later = i + 1 + t
                if t < NEAR:
                    @pl.when(jnp.logical_and(i > 0, later < blocks))
                    def _():
                        lower_step(later, i - 1)
                else:
                    @pl.when(jnp.logical_and(i >= t, i + 2 < blocks))
                    def _():
                        lower_step(i + 2, i - t)

        def places(first, last):
            @pl.when(i == 0)
            def _():
                for t in range(first, last):
                    place(t)

        def residual(a):
            finish(across_copies(i, a))
            total = px[a]
            for s in range(n_x - 1):
                total = total + x_in[parity, a, s]
            turned = [turn(total, d) for d in range(GROUPS)]
            spread = [
                by_group([turned[(g - b) % GROUPS] for g in range(GROUPS)])
                for b in range(GROUPS)
            ]
            eb[a] = halves(jnp.concatenate(spread, axis=0), 1)

        def diag_chunk(a, q):
            rows = span // CHUNKS
            value = product(db[q], eb[a])
            value = by_group([
                value[(h * CORES + v) * rows:(h * CORES + v + 1) * rows]
                for v in range(CORES) for h in range(CHAINS)
            ])
            at = (a * CHUNKS + q) * n_own
            part[at:at + n_own] = value.reshape(n_own, strip, rotor)

        @pl.when(i < blocks - 1)
        def _():
            for a in range(CHAINS):
                residual(a)
                for q in range(CHUNKS):
                    diag_chunk(a, q)
                    for t in range(n_own):
                        @pl.when(owner_away[t])
                        def _():
                            reduce_copy(a * CHUNKS + q, t).start()
            prepare_lower(pair_index(i + 1, i))
            deferred(*range(TURNS))
            places(1, 4)

            @pl.when(is_owner)
            def _():
                for q in range(CHAINS * CHUNKS):
                    at = q * n_own + me_owner
                    total = part[at]
                    for s in range(1, n_row):
                        reduce_arrival(q, s).wait_recv()
                    for s in range(1, n_row):
                        total = total + rs_in[row_at[s], q]
                    ysh[at] = total
                    for s in reversed(range(1, n_row)):
                        gather_copy(q, s).start()

            deferred(*range(TURNS, blocks - 2))
            places(4, blocks)
            prepare_diag(i + 1)
            for a in range(CHAINS):
                for q in range(a * CHUNKS, (a + 1) * CHUNKS):
                    for t in range(n_own):
                        @pl.when(owner_away[t])
                        def _():
                            gather_arrival(q, t).wait_recv()
                value = ysh[a * strips:(a + 1) * strips].reshape(span, rotor)
                yb[a] = halves(value, 1)
                send_across(i + 1, a, [product(lb[h], yb[a]) for h in range(CHAINS)])
            chains = [
                ysh[a * strips:(a + 1) * strips].reshape(span, rotor) for a in range(CHAINS)
            ]
            for h in range(CHAINS):
                value = arranged(chains, h)
                whole[h * span:(h + 1) * span] = value
                yd[i, h * span:(h + 1) * span] = halves(value, 1)
            own[i] = whole[pl.ds(r * piece, piece)]
            for q in range(CHAINS * CHUNKS):
                for t in range(n_own):
                    @pl.when(owner_away[t])
                    def _():
                        reduce_copy(q, t).wait_send()

            @pl.when(is_owner)
            def _():
                for q in range(CHAINS * CHUNKS):
                    for s in range(1, n_row):
                        gather_copy(q, s).wait_send()

        @pl.when(i == blocks - 1)
        def _():
            earlier = own_copy(0, blocks - 1, 0)
            earlier.start()
            for a in range(CHAINS):
                residual(a)
                for q in range(CHUNKS):
                    diag_chunk(a, q)
            for g in range(n_row):
                at = g % (n_row // CHAINS) * per_piece
                chains = [
                    part[a * strips + at:a * strips + at + per_piece].reshape(piece, rotor)
                    for a in range(CHAINS)
                ]
                last[g] = arranged(chains, g // (n_row // CHAINS))

                @pl.when(g != r)
                def _():
                    final_copy(g).start()
            earlier.wait()
            for j in range(blocks - 1):
                write_out(j)
            total = last[r]
            for s in range(1, n_row):
                final_arrival(s).wait_recv()
                total = total + fin_in[row_at[s]]
            own[blocks - 1] = total
            latest = own_copy(blocks - 1, 1, 1)
            latest.start()
            latest.wait()
            write_out(blocks - 1)
            for g in range(n_row):
                @pl.when(g != r)
                def _():
                    final_copy(g).wait_send()

        return carry

    for a in range(CHAINS):
        send_across(0, a)
    prepare_diag(0)
    lax.fori_loop(0, blocks, step, 0)


def per_device(
    sub_field, reluctivity, stride, counts, source_cell, target_row, lower_tiles, diag_inverse
):
    n_row, n_col = lax.axis_size("row"), lax.axis_size("col")
    blocks, tile_rows, rotor = diag_inverse.shape[0], lower_tiles.shape[1], sub_field.shape[1]
    cap = source_cell.shape[2]
    pairs = lower_tiles.shape[0]
    share = diag_inverse.shape[1]
    piece = share // n_row
    n_x = n_col // CORES
    n_own = n_row // 2
    strips = CHAINS * CHUNKS * n_own
    strip = share // strips
    f32 = jnp.float32
    bf16 = jnp.bfloat16
    vmem = pl.BlockSpec(memory_space=pltpu.VMEM)
    hbm = pl.BlockSpec(memory_space=pltpu.HBM)
    dma = pltpu.SemaphoreType.DMA
    pieces = pl.pallas_call(
        functools.partial(solve_kernel, n_row, n_col),
        out_shape=jax.ShapeDtypeStruct((blocks, piece, rotor), f32),
        in_specs=[pl.BlockSpec(memory_space=pltpu.SMEM)] + [hbm] * 7,
        out_specs=vmem,
        scratch_shapes=[
            pltpu.SMEM(counts.shape, jnp.int32),
            pltpu.SMEM(source_cell.shape, jnp.int32),
            pltpu.VMEM((CORES, n_row, cap), jnp.int32),
            pltpu.VMEM(sub_field.shape, f32),
            pltpu.VMEM(reluctivity.shape, f32),
            pltpu.VMEM((n_row, cap, rotor), f32),
            pltpu.VMEM((n_row, CORES, cap // 2, rotor), f32),
            pltpu.VMEM((n_row * CORES, cap // 2, rotor), f32),
            pltpu.VMEM((n_row * cap, 2 * rotor), bf16),
            pltpu.VMEM((2, tile_rows, n_row * cap), bf16),
            pltpu.VMEM((pairs, CORES) + lower_tiles.shape[1:], f32),
            pltpu.VMEM((blocks, CORES) + diag_inverse.shape[1:], f32),
            pltpu.VMEM((CHAINS, CORES * tile_rows, 2 * share // CHAINS), bf16),
            pltpu.VMEM((CHUNKS, CORES * share // CHUNKS, 2 * tile_rows), bf16),
            pltpu.VMEM((blocks, tile_rows, rotor), f32),
            pltpu.VMEM((CHAINS, tile_rows // GROUPS, rotor), f32),
            pltpu.VMEM((2, CHAINS, n_x - 1, tile_rows // GROUPS, rotor), f32),
            pltpu.VMEM((CHAINS, tile_rows, 2 * rotor), bf16),
            pltpu.VMEM((strips, strip, rotor), f32),
            pltpu.VMEM((n_row, CHAINS * CHUNKS, strip, rotor), f32),
            pltpu.VMEM((strips, strip, rotor), f32),
            pltpu.VMEM((CHAINS, share // CHAINS, 2 * rotor), bf16),
            pltpu.VMEM((blocks, share, 2 * rotor), bf16),
            pltpu.VMEM((share, rotor), f32),
            pltpu.VMEM((n_row, piece, rotor), f32),
            pltpu.VMEM((n_row, piece, rotor), f32),
            pltpu.VMEM((blocks, piece, rotor), f32),
            pltpu.VMEM((blocks, piece, rotor), f32),
            dma((5,)),
            dma((2, 1)),
            dma((2, n_row, CORES)),
            dma((pairs,)),
            dma((blocks,)),
            dma((2, pairs)),
            dma((2, blocks)),
            dma((2, 2, CHAINS, n_x - 1)),
            dma((CHAINS * CHUNKS, n_own)),
            dma((n_row, CHAINS * CHUNKS)),
            dma((CHAINS * CHUNKS, n_row - 1)),
            dma((strips,)),
            dma((n_row,)),
            dma((n_row,)),
            dma((2, 2)),
        ],
        compiler_params=pltpu.CompilerParams(
            collective_id=0, has_side_effects=True, vmem_limit_bytes=67043328
        ),
    )(
        stride, counts, source_cell, target_row, sub_field, reluctivity, lower_tiles, diag_inverse
    )
    return pieces[:, None]


def solution(mesh):
    placed = (
        P(("row", "col"), None),
        P(None, ("row", "col"), None),
        P(("row", "col")),
        P(("row", "col"), None),
        P(("row", "col"), None, None),
        P("row", "col", None, None),
        P(None, "row", "col"),
        P(None, "col", "row"),
    )
    return jax.shard_map(
        per_device,
        mesh=mesh,
        in_specs=placed,
        out_specs=P(None, "col", "row", None),
        check_vma=False,
    )
```

```python
import functools

import jax
import jax.numpy as jnp
from jax import lax
from jax.experimental import pallas as pl
from jax.experimental.pallas import tpu as pltpu
from jax.sharding import PartitionSpec as P

MESH = pl.DeviceIdType.MESH
CORES = 2
PICKS = 8
CHAINS = 2
GROUPS = 2 * CHAINS
CHUNKS = 2
DEPTH = 4
TURNS = 2
NEAR = 4


def pair_index(later_block, earlier_block):
    return later_block * (later_block - 1) // 2 + earlier_block


def halves(value, axis):
    high = value.astype(jnp.bfloat16)
    low = (value - high.astype(jnp.float32)).astype(jnp.bfloat16)
    return jnp.concatenate([high, low], axis=axis)


def product(left_halves, right_halves):
    rotor = right_halves.shape[1] // 2
    right = jnp.concatenate([right_halves, right_halves], axis=0)
    full = jnp.dot(left_halves, right, preferred_element_type=jnp.float32)
    return full[:, :rotor] + full[:, rotor:]


def turn(value, groups):
    width = value.shape[1] // GROUPS
    return pltpu.roll(value, groups % GROUPS * width, 1) if groups % GROUPS else value


def group_of(shape):
    return lax.broadcasted_iota(jnp.int32, shape, 1) // (shape[1] // GROUPS)


def by_group(values):
    group = group_of(values[0].shape)

    def among(first, last):
        if last - first == 1:
            return values[first]
        middle = (first + last) // 2
        return jnp.where(group < middle, among(first, middle), among(middle, last))

    return among(0, len(values))


def arranged(chains, part):
    return by_group([turn(chains[g % CHAINS], g % CHAINS - part) for g in range(GROUPS)])


def swap_lanes(value):
    return turn(value, GROUPS // 2)


def solve_kernel(
    n_row, n_col, stride, counts_hbm, source_hbm, target_hbm, field_hbm, nu_hbm, lower_hbm,
    diag_hbm, out_ref, counts, source, target_rows, field, nu, picked, packs, received, arrived, spot,
    lower, diag, lb, db, acc, px, x_in, eb, part, rs_in, ysh, yb, yd, whole, last, fin_in, own, theirs,
    f_sem, t_sems, p_sems, w_sem, d_sem, wr_sems, dr_sems, x_sems, rs_send, rs_recv, ag_send, ag_recv, fin_send,
    fin_recv, o_sems,
):
    blocks, _, share, tile_rows = diag.shape
    rotor = px.shape[2]
    n_x = n_col // CORES
    n_y = n_row // DEPTH
    first_owner, n_own = n_y, n_row // 2
    strip = part.shape[1]
    strips = part.shape[0] // CHAINS
    piece = share // n_row
    per_piece = piece // strip
    r = lax.axis_index("row")
    c = lax.axis_index("col")
    core = lax.rem(c, CORES)
    other = 1 - core
    c_other = c + 1 - 2 * core
    core_peer = {"col": c_other}
    x_peer = [{"col": lax.rem(c + CORES * s, n_col)} for s in range(1, n_x)]
    row_at = [lax.rem(r + s, n_row) for s in range(n_row)]
    cols_at = [c, c_other]
    far_first = sorted(range(1, n_row), key=lambda s: -min(s, n_row - s))
    peers = [{"row": row_at[s], "col": k} for s in far_first for k in cols_at]
    peers += x_peer + [core_peer]
    slots = source.shape[2]
    half_slots = slots // 2
    span = share // CHAINS
    quarter = tile_rows // GROUPS
    is_owner = jnp.logical_and(r >= first_owner, r < first_owner + n_own)
    me_owner = jnp.clip(r - first_owner, 0, n_own - 1)
    owner_at = [lax.rem(r + n_own // 2 + n_own - t, n_own) for t in range(n_own)]
    owner_away = [first_owner + o != r for o in owner_at]

    def first_half(shape):
        return lax.broadcasted_iota(jnp.int32, shape, 1) < rotor // 2

    def merge(left, right):
        return jnp.where(first_half(left.shape), left, right)

    def between(src, dst, send, recv, device):
        return pltpu.make_async_remote_copy(
            src_ref=src, dst_ref=dst, send_sem=send, recv_sem=recv,
            device_id=device, device_id_type=MESH,
        )

    def describe(src, dst, sems, at, device):
        return between(src, dst, sems.at[(0,) + at], sems.at[(1,) + at], device)

    def remote(src, dst, sems, at, device):
        copy = describe(src, dst, sems, at, device)
        copy.start()
        return copy

    def load_lower(k):
        return pltpu.make_async_copy(lower_hbm.at[k], lower.at[k, core], w_sem.at[k])

    def share_lower(k):
        return describe(lower_hbm.at[k], lower.at[k, core], wr_sems, (k,), core_peer)

    def load_diag(k):
        return pltpu.make_async_copy(diag_hbm.at[k], diag.at[k, core], d_sem.at[k])

    def share_diag(k):
        return describe(diag_hbm.at[k], diag.at[k, core], dr_sems, (k,), core_peer)

    def finish(copies):
        for copy in copies:
            copy.wait()

    loads = (
        pltpu.make_async_copy(counts_hbm, counts, f_sem.at[3]),
        pltpu.make_async_copy(source_hbm, source, f_sem.at[4]),
        pltpu.make_async_copy(target_hbm.at[0, 0], target_rows.at[core], f_sem.at[2]),
        pltpu.make_async_copy(field_hbm, field, f_sem.at[0]),
        pltpu.make_async_copy(nu_hbm, nu, f_sem.at[1]),
    )
    barrier = pltpu.get_barrier_semaphore()
    for p in peers:
        pl.semaphore_signal(barrier, inc=1, device_id=p, device_id_type=MESH)
    for copy in loads:
        copy.start()

    def pick(s):
        g = row_at[s]
        band = stride[0]
        live_slots = counts[0, g]

        def group(k8, carry):
            for u in range(PICKS):
                k = k8 * PICKS + u
                m = source[0, g, k]
                here = field[pl.ds(m, 1), :]
                radial = field[pl.ds(jnp.maximum(m - band, 0), 1), :]
                tangent = field[pl.ds(jnp.maximum(m - 1, 0), 1), :]
                has_radial = jnp.where(m >= band, 1.0, 0.0)
                has_tangent = jnp.where(m >= 1, 1.0, 0.0)
                live = jnp.where(k < live_slots, 1.0, 0.0)
                swept = nu[0, pl.ds(m, 1), :] * (here - radial * has_radial) + nu[
                    1, pl.ds(m, 1), :
                ] * (here - tangent * has_tangent)
                picked[s, pl.ds(k, 1), :] = swept * live
            return carry

        lax.fori_loop(0, slots // PICKS, group, 0)
        early, late = picked[s, :half_slots], picked[s, half_slots:]
        packs[s, 0] = merge(early, swap_lanes(late))
        packs[s, 1] = merge(swap_lanes(early), late)

    for copy in loads:
        copy.wait()
    mine = r * CORES + core
    order = [("d", 0)]
    for j in range(blocks - 1):
        order += [("l", pair_index(j + 1, j)), ("d", j + 1)]
        order += [("l", pair_index(i, j)) for i in range(j + 2, blocks)]
    for kind, k in order:
        (load_diag(k) if kind == "d" else load_lower(k)).start()
    sent = []
    for s in list(range(1, n_row)) + [0]:
        pick(s)
        if s == 1:
            pl.semaphore_wait(barrier, len(peers))
            targets_sent = remote(
                target_rows.at[core], target_rows.at[core], t_sems, (0,), core_peer
            )
        for w, (k, col) in enumerate(((core, c), (other, c_other))):
            if s or w:
                sent.append(remote(
                    packs.at[s, k], received.at[mine], p_sems, (s, w), {"row": row_at[s], "col": col},
                ))
    for kind, k in order:
        (share_diag(k) if kind == "d" else share_lower(k)).start()
    received[mine] = packs[0, core]
    targets_sent.wait()
    targets = [
        jnp.concatenate(
            [
                target_rows[k, q:q + 1, h * half_slots:(h + 1) * half_slots]
                for q in range(n_row) for k in range(CORES)
            ],
            axis=1,
        )
        for h in range(2)
    ]

    def chosen(i, h):
        here = lax.broadcasted_iota(jnp.int32, (tile_rows, arrived.shape[0]), 0) + i * tile_rows
        return jnp.where(here == targets[h], 1.0, 0.0).astype(jnp.bfloat16)

    def place(i, rows=None):
        sums = []
        for h in range(2):
            full = jnp.dot(
                rows[h] if rows else chosen(i, h), arrived[...],
                preferred_element_type=jnp.float32,
            )
            sums.append(full[:, :rotor] + full[:, rotor:])
        acc[i] = merge(*sums)

    for h in range(2):
        spot[h] = chosen(0, h)
    finish(sent)
    arrived[...] = halves(received[...].reshape(arrived.shape[0], rotor), 1)
    place(0, [spot[h] for h in range(2)])

    def lower_half(k, h):
        return lower[k, :, :, h * span:(h + 1) * span].reshape(
            CORES * tile_rows, span
        )

    def lower_step(i, j):
        k = pair_index(i, j)
        finish([load_lower(k), share_lower(k)])
        left = halves(lower[k].reshape(CORES * tile_rows, share), 1)
        value = product(left, yd[j])
        acc[i] = acc[i] - merge(value[:tile_rows], value[tile_rows:])

    def prepare_lower(k):
        finish([load_lower(k), share_lower(k)])
        for h in range(CHAINS):
            lb[h] = halves(lower_half(k, h), 1)

    def prepare_diag(i):
        finish([load_diag(i), share_diag(i)])
        rows = span // CHUNKS
        for q in range(CHUNKS):
            for h in range(CHAINS):
                at = h * span + q * rows
                db[q, h * CORES * rows:(h + 1) * CORES * rows] = halves(
                    diag[i, :, at:at + rows].reshape(CORES * rows, tile_rows), 1
                )

    def across_copies(i, a):
        parity = lax.rem(i, 2)
        return [
            describe(px.at[a], x_in.at[parity, a, s], x_sems, (parity, a, s), p)
            for s, p in enumerate(x_peer)
        ]

    def send_across(i, a, products=None):
        value = acc[i]
        value = jnp.where(lax.rem(group_of(value.shape), CHAINS) == a, value, 0.0)
        if products:
            value = value - by_group([
                products[h][v * tile_rows:(v + 1) * tile_rows]
                for v in range(CORES) for h in range(CHAINS)
            ])
        rows = [value[b * quarter:(b + 1) * quarter] for b in range(GROUPS)]
        px[a] = sum(
            turn(by_group([rows[(g - d) % GROUPS] for g in range(GROUPS)]), -d)
            for d in range(GROUPS)
        )
        for copy in across_copies(i, a):
            copy.start()

    def reduce_copy(q, t):
        o = owner_at[t]
        return between(
            part.at[q * n_own + o], rs_in.at[r, q], rs_send.at[q, t], rs_recv.at[r, q],
            {"row": first_owner + o},
        )

    def reduce_arrival(q, s):
        src = row_at[s]
        return between(
            part.at[q], rs_in.at[src, q], rs_send.at[q, 0], rs_recv.at[src, q], {"row": src}
        )

    def gather_copy(q, s):
        at = q * n_own + me_owner
        return between(
            ysh.at[at], ysh.at[at], ag_send.at[q, s - 1], ag_recv.at[at], {"row": row_at[s]}
        )

    def gather_arrival(q, t):
        at = q * n_own + owner_at[t]
        return between(
            ysh.at[at], ysh.at[at], ag_send.at[q, 0], ag_recv.at[at],
            {"row": first_owner + owner_at[t]},
        )

    def final_copy(g, w):
        return between(
            last.at[g, w], fin_in.at[r, core], fin_send.at[g, w], fin_recv.at[r, core],
            {"row": g, "col": c - core + w},
        )

    def final_arrival(s, w):
        src = row_at[s]
        return between(
            last.at[0, 0], fin_in.at[src, w], fin_send.at[0, 0], fin_recv.at[src, w],
            {"row": src, "col": c - core + w},
        )

    def own_copy(first, count, at):
        span = pl.ds(first, count)
        return describe(own.at[span], theirs.at[span], o_sems, (at,), core_peer)

    def write_out(i):
        swapped = swap_lanes(theirs[i])
        low, high = merge(own[i], swapped), merge(swapped, own[i])
        out_ref[i] = jnp.where(core == 0, low, high)

    def step(i, carry):
        parity = lax.rem(i, 2)

        def deferred(*turns):
            for t in turns:
                later = i + 1 + t
                if t < NEAR:
                    @pl.when(jnp.logical_and(i > 0, later < blocks))
                    def _():
                        lower_step(later, i - 1)
                else:
                    @pl.when(jnp.logical_and(i >= t, i + 2 < blocks))
                    def _():
                        lower_step(i + 2, i - t)

        def places(first, last):
            @pl.when(i == 0)
            def _():
                for t in range(first, last):
                    place(t)

        def residual(a):
            finish(across_copies(i, a))
            total = px[a]
            for s in range(n_x - 1):
                total = total + x_in[parity, a, s]
            turned = [turn(total, d) for d in range(GROUPS)]
            spread = [
                by_group([turned[(g - b) % GROUPS] for g in range(GROUPS)])
                for b in range(GROUPS)
            ]
            eb[a] = halves(jnp.concatenate(spread, axis=0), 1)

        def diag_chunk(a, q):
            rows = span // CHUNKS
            value = product(db[q], eb[a])
            value = by_group([
                value[(h * CORES + v) * rows:(h * CORES + v + 1) * rows]
                for v in range(CORES) for h in range(CHAINS)
            ])
            at = (a * CHUNKS + q) * n_own
            part[at:at + n_own] = value.reshape(n_own, strip, rotor)

        @pl.when(i < blocks - 1)
        def _():
            for a in range(CHAINS):
                residual(a)
                for q in range(CHUNKS):
                    diag_chunk(a, q)
                    for t in range(n_own):
                        @pl.when(owner_away[t])
                        def _():
                            reduce_copy(a * CHUNKS + q, t).start()
            prepare_lower(pair_index(i + 1, i))
            deferred(*range(TURNS))
            places(1, 4)

            @pl.when(is_owner)
            def _():
                for q in range(CHAINS * CHUNKS):
                    at = q * n_own + me_owner
                    total = part[at]
                    for s in range(1, n_row):
                        reduce_arrival(q, s).wait_recv()
                        total = total + rs_in[row_at[s], q]
                    ysh[at] = total
                    for s in reversed(range(1, n_row)):
                        gather_copy(q, s).start()

            deferred(*range(TURNS, blocks - 2))
            places(4, blocks)
            prepare_diag(i + 1)
            for a in range(CHAINS):
                for q in range(a * CHUNKS, (a + 1) * CHUNKS):
                    for t in range(n_own):
                        @pl.when(owner_away[t])
                        def _():
                            gather_arrival(q, t).wait_recv()
                value = ysh[a * strips:(a + 1) * strips].reshape(span, rotor)
                yb[a] = halves(value, 1)
                send_across(i + 1, a, [product(lb[h], yb[a]) for h in range(CHAINS)])
            chains = [
                ysh[a * strips:(a + 1) * strips].reshape(span, rotor) for a in range(CHAINS)
            ]
            for h in range(CHAINS):
                value = arranged(chains, h)
                whole[h * span:(h + 1) * span] = value
                yd[i, h * span:(h + 1) * span] = halves(value, 1)
            own[i] = whole[pl.ds(r * piece, piece)]
            for q in range(CHAINS * CHUNKS):
                for t in range(n_own):
                    @pl.when(owner_away[t])
                    def _():
                        reduce_copy(q, t).wait_send()

            @pl.when(is_owner)
            def _():
                for q in range(CHAINS * CHUNKS):
                    for s in range(1, n_row):
                        gather_copy(q, s).wait_send()

        @pl.when(i == blocks - 1)
        def _():
            earlier = own_copy(0, blocks - 1, 0)
            earlier.start()
            for a in range(CHAINS):
                residual(a)
                for q in range(CHUNKS):
                    diag_chunk(a, q)
            for g in range(n_row):
                at = g % (n_row // CHAINS) * per_piece
                chains = [
                    part[a * strips + at:a * strips + at + per_piece].reshape(piece, rotor)
                    for a in range(CHAINS)
                ]
                value = arranged(chains, g // (n_row // CHAINS))
                upper, lower_rows = value[:piece // 2], value[piece // 2:]
                last[g, 0] = merge(upper, swap_lanes(lower_rows))
                last[g, 1] = merge(swap_lanes(upper), lower_rows)
                for w in range(CORES):
                    @pl.when(jnp.logical_or(g != r, w != core))
                    def _():
                        final_copy(g, w).start()
            earlier.wait()
            for j in range(blocks - 1):
                write_out(j)
            fin_in[r, core] = last[r, core]
            for s in list(range(1, n_row)) + [0]:
                for w in range(CORES):
                    @pl.when(jnp.logical_or(s != 0, w != core))
                    def _():
                        final_arrival(s, w).wait_recv()
            left, right = (sum(fin_in[g, w] for g in range(n_row)) for w in range(CORES))
            out_ref[blocks - 1, :piece // 2] = merge(left, swap_lanes(right))
            out_ref[blocks - 1, piece // 2:] = merge(swap_lanes(left), right)
            for g in range(n_row):
                for w in range(CORES):
                    @pl.when(jnp.logical_or(g != r, w != core))
                    def _():
                        final_copy(g, w).wait_send()

        return carry

    for a in range(CHAINS):
        send_across(0, a)
    prepare_diag(0)
    lax.fori_loop(0, blocks, step, 0)


def per_device(
    sub_field, reluctivity, stride, counts, source_cell, target_row, lower_tiles, diag_inverse
):
    n_row, n_col = lax.axis_size("row"), lax.axis_size("col")
    blocks, tile_rows, rotor = diag_inverse.shape[0], lower_tiles.shape[1], sub_field.shape[1]
    cap = source_cell.shape[2]
    pairs = lower_tiles.shape[0]
    share = diag_inverse.shape[1]
    piece = share // n_row
    n_x = n_col // CORES
    n_own = n_row // 2
    strips = CHAINS * CHUNKS * n_own
    strip = share // strips
    f32 = jnp.float32
    bf16 = jnp.bfloat16
    vmem = pl.BlockSpec(memory_space=pltpu.VMEM)
    hbm = pl.BlockSpec(memory_space=pltpu.HBM)
    dma = pltpu.SemaphoreType.DMA
    pieces = pl.pallas_call(
        functools.partial(solve_kernel, n_row, n_col),
        out_shape=jax.ShapeDtypeStruct((blocks, piece, rotor), f32),
        in_specs=[pl.BlockSpec(memory_space=pltpu.SMEM)] + [hbm] * 7,
        out_specs=vmem,
        scratch_shapes=[
            pltpu.SMEM(counts.shape, jnp.int32),
            pltpu.SMEM(source_cell.shape, jnp.int32),
            pltpu.VMEM((CORES, n_row, cap), jnp.int32),
            pltpu.VMEM(sub_field.shape, f32),
            pltpu.VMEM(reluctivity.shape, f32),
            pltpu.VMEM((n_row, cap, rotor), f32),
            pltpu.VMEM((n_row, CORES, cap // 2, rotor), f32),
            pltpu.VMEM((n_row * CORES, cap // 2, rotor), f32),
            pltpu.VMEM((n_row * cap, 2 * rotor), bf16),
            pltpu.VMEM((2, tile_rows, n_row * cap), bf16),
            pltpu.VMEM((pairs, CORES) + lower_tiles.shape[1:], f32),
            pltpu.VMEM((blocks, CORES) + diag_inverse.shape[1:], f32),
            pltpu.VMEM((CHAINS, CORES * tile_rows, 2 * share // CHAINS), bf16),
            pltpu.VMEM((CHUNKS, CORES * share // CHUNKS, 2 * tile_rows), bf16),
            pltpu.VMEM((blocks, tile_rows, rotor), f32),
            pltpu.VMEM((CHAINS, tile_rows // GROUPS, rotor), f32),
            pltpu.VMEM((2, CHAINS, n_x - 1, tile_rows // GROUPS, rotor), f32),
            pltpu.VMEM((CHAINS, tile_rows, 2 * rotor), bf16),
            pltpu.VMEM((strips, strip, rotor), f32),
            pltpu.VMEM((n_row, CHAINS * CHUNKS, strip, rotor), f32),
            pltpu.VMEM((strips, strip, rotor), f32),
            pltpu.VMEM((CHAINS, share // CHAINS, 2 * rotor), bf16),
            pltpu.VMEM((blocks, share, 2 * rotor), bf16),
            pltpu.VMEM((share, rotor), f32),
            pltpu.VMEM((n_row, CORES, piece // 2, rotor), f32),
            pltpu.VMEM((n_row, CORES, piece // 2, rotor), f32),
            pltpu.VMEM((blocks, piece, rotor), f32),
            pltpu.VMEM((blocks, piece, rotor), f32),
            dma((5,)),
            dma((2, 1)),
            dma((2, n_row, CORES)),
            dma((pairs,)),
            dma((blocks,)),
            dma((2, pairs)),
            dma((2, blocks)),
            dma((2, 2, CHAINS, n_x - 1)),
            dma((CHAINS * CHUNKS, n_own)),
            dma((n_row, CHAINS * CHUNKS)),
            dma((CHAINS * CHUNKS, n_row - 1)),
            dma((strips,)),
            dma((n_row, CORES)),
            dma((n_row, CORES)),
            dma((2, 1)),
        ],
        compiler_params=pltpu.CompilerParams(
            collective_id=0, has_side_effects=True, vmem_limit_bytes=67043328
        ),
    )(
        stride, counts, source_cell, target_row, sub_field, reluctivity, lower_tiles, diag_inverse
    )
    return pieces[:, None]


def solution(mesh):
    placed = (
        P(("row", "col"), None),
        P(None, ("row", "col"), None),
        P(("row", "col")),
        P(("row", "col"), None),
        P(("row", "col"), None, None),
        P("row", "col", None, None),
        P(None, "row", "col"),
        P(None, "col", "row"),
    )
    return jax.shard_map(
        per_device,
        mesh=mesh,
        in_specs=placed,
        out_specs=P(None, "col", "row", None),
        check_vma=False,
    )
```

```python
import functools

import jax
import jax.numpy as jnp
from jax import lax
from jax.experimental import pallas as pl
from jax.experimental.pallas import tpu as pltpu
from jax.sharding import PartitionSpec as P

MESH = pl.DeviceIdType.MESH
CORES = 2
PICKS = 8
CHAINS = 2
GROUPS = 2 * CHAINS
CHUNKS = 2
DEPTH = 4
TURNS = 1
NEAR = 4


def pair_index(later_block, earlier_block):
    return later_block * (later_block - 1) // 2 + earlier_block


def halves(value, axis):
    high = value.astype(jnp.bfloat16)
    low = (value - high.astype(jnp.float32)).astype(jnp.bfloat16)
    return jnp.concatenate([high, low], axis=axis)


def product(left_halves, right_halves):
    rotor = right_halves.shape[1] // 2
    right = jnp.concatenate([right_halves, right_halves], axis=0)
    full = jnp.dot(left_halves, right, preferred_element_type=jnp.float32)
    return full[:, :rotor] + full[:, rotor:]


def turn(value, groups):
    width = value.shape[1] // GROUPS
    return pltpu.roll(value, groups % GROUPS * width, 1) if groups % GROUPS else value


def group_of(shape):
    return lax.broadcasted_iota(jnp.int32, shape, 1) // (shape[1] // GROUPS)


def by_group(values):
    group = group_of(values[0].shape)

    def among(first, last):
        if last - first == 1:
            return values[first]
        middle = (first + last) // 2
        return jnp.where(group < middle, among(first, middle), among(middle, last))

    return among(0, len(values))


def arranged(chains, part):
    return by_group([turn(chains[g % CHAINS], g % CHAINS - part) for g in range(GROUPS)])


def swap_lanes(value):
    return turn(value, GROUPS // 2)


def solve_kernel(
    n_row, n_col, stride, counts_hbm, source_hbm, target_hbm, field_hbm, nu_hbm, lower_hbm,
    diag_hbm, out_ref, counts, source, target_rows, field, nu, picked, packs, received, arrived, spot,
    lower, diag, lb, db, acc, px, x_in, eb, part, rs_in, ysh, yd, whole, last, fin_in, own, theirs,
    f_sem, t_sems, p_sems, w_sem, d_sem, wr_sems, dr_sems, x_sems, rs_send, rs_recv, ag_send, ag_recv, fin_send,
    fin_recv, o_sems,
):
    blocks, _, share, tile_rows = diag.shape
    rotor = px.shape[2]
    n_x = n_col // CORES
    n_y = n_row // DEPTH
    first_owner, n_own = n_y, n_row // 2
    strip = part.shape[1]
    strips = part.shape[0] // CHAINS
    piece = share // n_row
    per_piece = piece // strip
    r = lax.axis_index("row")
    c = lax.axis_index("col")
    core = lax.rem(c, CORES)
    other = 1 - core
    c_other = c + 1 - 2 * core
    core_peer = {"col": c_other}
    x_peer = [{"col": lax.rem(c + CORES * s, n_col)} for s in range(1, n_x)]
    row_at = [lax.rem(r + s, n_row) for s in range(n_row)]
    cols_at = [c, c_other]
    far_first = sorted(range(1, n_row), key=lambda s: -min(s, n_row - s))
    peers = [{"row": row_at[s], "col": k} for s in far_first for k in cols_at]
    peers += x_peer + [core_peer]
    slots = source.shape[2]
    half_slots = slots // 2
    span = share // CHAINS
    quarter = tile_rows // GROUPS
    is_owner = jnp.logical_and(r >= first_owner, r < first_owner + n_own)
    me_owner = jnp.clip(r - first_owner, 0, n_own - 1)
    owner_at = [lax.rem(r + n_own // 2 + n_own - t, n_own) for t in range(n_own)]
    owner_away = [first_owner + o != r for o in owner_at]

    def first_half(shape):
        return lax.broadcasted_iota(jnp.int32, shape, 1) < rotor // 2

    def merge(left, right):
        return jnp.where(first_half(left.shape), left, right)

    def between(src, dst, send, recv, device):
        return pltpu.make_async_remote_copy(
            src_ref=src, dst_ref=dst, send_sem=send, recv_sem=recv,
            device_id=device, device_id_type=MESH,
        )

    def describe(src, dst, sems, at, device):
        return between(src, dst, sems.at[(0,) + at], sems.at[(1,) + at], device)

    def remote(src, dst, sems, at, device):
        copy = describe(src, dst, sems, at, device)
        copy.start()
        return copy

    def load_lower(k):
        return pltpu.make_async_copy(lower_hbm.at[k], lower.at[k, core], w_sem.at[k])

    def share_lower(k):
        return describe(lower_hbm.at[k], lower.at[k, core], wr_sems, (k,), core_peer)

    def load_diag(k):
        return pltpu.make_async_copy(diag_hbm.at[k], diag.at[k, core], d_sem.at[k])

    def share_diag(k):
        return describe(diag_hbm.at[k], diag.at[k, core], dr_sems, (k,), core_peer)

    def finish(copies):
        for copy in copies:
            copy.wait()

    loads = (
        pltpu.make_async_copy(counts_hbm, counts, f_sem.at[3]),
        pltpu.make_async_copy(source_hbm, source, f_sem.at[4]),
        pltpu.make_async_copy(target_hbm.at[0, 0], target_rows.at[core], f_sem.at[2]),
        pltpu.make_async_copy(field_hbm, field, f_sem.at[0]),
        pltpu.make_async_copy(nu_hbm, nu, f_sem.at[1]),
    )
    barrier = pltpu.get_barrier_semaphore()
    for p in peers:
        pl.semaphore_signal(barrier, inc=1, device_id=p, device_id_type=MESH)
    for copy in loads:
        copy.start()

    def pick(s):
        g = row_at[s]
        band = stride[0]
        live_slots = counts[0, g]

        def group(k8, carry):
            for u in range(PICKS):
                k = k8 * PICKS + u
                m = source[0, g, k]
                here = field[pl.ds(m, 1), :]
                radial = field[pl.ds(jnp.maximum(m - band, 0), 1), :]
                tangent = field[pl.ds(jnp.maximum(m - 1, 0), 1), :]
                has_radial = jnp.where(m >= band, 1.0, 0.0)
                has_tangent = jnp.where(m >= 1, 1.0, 0.0)
                live = jnp.where(k < live_slots, 1.0, 0.0)
                swept = nu[0, pl.ds(m, 1), :] * (here - radial * has_radial) + nu[
                    1, pl.ds(m, 1), :
                ] * (here - tangent * has_tangent)
                picked[s, pl.ds(k, 1), :] = swept * live
            return carry

        lax.fori_loop(0, slots // PICKS, group, 0)
        early, late = picked[s, :half_slots], picked[s, half_slots:]
        packs[s, 0] = merge(early, swap_lanes(late))
        packs[s, 1] = merge(swap_lanes(early), late)

    for copy in loads:
        copy.wait()
    mine = r * CORES + core
    order = [("d", 0)]
    for j in range(blocks - 1):
        order += [("l", pair_index(j + 1, j)), ("d", j + 1)]
        order += [("l", pair_index(i, j)) for i in range(j + 2, blocks)]
    for kind, k in order:
        (load_diag(k) if kind == "d" else load_lower(k)).start()
    sent = []
    for s in list(range(1, n_row)) + [0]:
        pick(s)
        if s == 1:
            pl.semaphore_wait(barrier, len(peers))
            targets_sent = remote(
                target_rows.at[core], target_rows.at[core], t_sems, (0,), core_peer
            )
        for w, (k, col) in enumerate(((core, c), (other, c_other))):
            if s or w:
                sent.append(remote(
                    packs.at[s, k], received.at[mine], p_sems, (s, w), {"row": row_at[s], "col": col},
                ))
    for kind, k in order:
        (share_diag(k) if kind == "d" else share_lower(k)).start()
    received[mine] = packs[0, core]
    targets_sent.wait()
    targets = [
        jnp.concatenate(
            [
                target_rows[k, q:q + 1, h * half_slots:(h + 1) * half_slots]
                for q in range(n_row) for k in range(CORES)
            ],
            axis=1,
        )
        for h in range(2)
    ]

    def chosen(i, h):
        here = lax.broadcasted_iota(jnp.int32, (tile_rows, arrived.shape[0]), 0) + i * tile_rows
        return jnp.where(here == targets[h], 1.0, 0.0).astype(jnp.bfloat16)

    def place(i, rows=None):
        sums = []
        for h in range(2):
            full = jnp.dot(
                rows[h] if rows else chosen(i, h), arrived[...],
                preferred_element_type=jnp.float32,
            )
            sums.append(full[:, :rotor] + full[:, rotor:])
        acc[i] = merge(*sums)

    for h in range(2):
        spot[h] = chosen(0, h)
    finish(sent)
    arrived[...] = halves(received[...].reshape(arrived.shape[0], rotor), 1)
    place(0, [spot[h] for h in range(2)])

    def lower_half(k, h):
        return lower[k, :, :, h * span:(h + 1) * span].reshape(
            CORES * tile_rows, span
        )

    def lower_step(i, j):
        k = pair_index(i, j)
        finish([load_lower(k), share_lower(k)])
        left = halves(lower[k].reshape(CORES * tile_rows, share), 1)
        value = product(left, yd[j])
        acc[i] = acc[i] - merge(value[:tile_rows], value[tile_rows:])

    def prepare_lower(k):
        finish([load_lower(k), share_lower(k)])
        for h in range(CHAINS):
            for q in range(CHUNKS):
                at = slice(q * span // CHUNKS, (q + 1) * span // CHUNKS)
                lb[h, q] = halves(lower_half(k, h)[:, at], 1)

    def prepare_diag(i):
        finish([load_diag(i), share_diag(i)])
        rows = span // CHUNKS
        for q in range(CHUNKS):
            for h in range(CHAINS):
                at = h * span + q * rows
                db[q, h * CORES * rows:(h + 1) * CORES * rows] = halves(
                    diag[i, :, at:at + rows].reshape(CORES * rows, tile_rows), 1
                )

    def across_copies(i, a):
        parity = lax.rem(i, 2)
        return [
            describe(px.at[a], x_in.at[parity, a, s], x_sems, (parity, a, s), p)
            for s, p in enumerate(x_peer)
        ]

    def send_across(i, a, products=None):
        value = acc[i]
        value = jnp.where(lax.rem(group_of(value.shape), CHAINS) == a, value, 0.0)
        if products:
            value = value - by_group([
                products[h][v * tile_rows:(v + 1) * tile_rows]
                for v in range(CORES) for h in range(CHAINS)
            ])
        rows = [value[b * quarter:(b + 1) * quarter] for b in range(GROUPS)]
        px[a] = sum(
            turn(by_group([rows[(g - d) % GROUPS] for g in range(GROUPS)]), -d)
            for d in range(GROUPS)
        )
        for copy in across_copies(i, a):
            copy.start()

    def reduce_copy(q, t):
        o = owner_at[t]
        return between(
            part.at[q * n_own + o], rs_in.at[r, q], rs_send.at[q, t], rs_recv.at[r, q],
            {"row": first_owner + o},
        )

    def reduce_arrival(q, s):
        src = row_at[s]
        return between(
            part.at[q], rs_in.at[src, q], rs_send.at[q, 0], rs_recv.at[src, q], {"row": src}
        )

    def gather_copy(q, s):
        at = q * n_own + me_owner
        return between(
            ysh.at[at], ysh.at[at], ag_send.at[q, s - 1], ag_recv.at[at], {"row": row_at[s]}
        )

    def gather_arrival(q, t):
        at = q * n_own + owner_at[t]
        return between(
            ysh.at[at], ysh.at[at], ag_send.at[q, 0], ag_recv.at[at],
            {"row": first_owner + owner_at[t]},
        )

    def final_copy(g, w):
        return between(
            last.at[g, w], fin_in.at[r, core], fin_send.at[g, w], fin_recv.at[r, core],
            {"row": g, "col": c - core + w},
        )

    def final_arrival(s, w):
        src = row_at[s]
        return between(
            last.at[0, 0], fin_in.at[src, w], fin_send.at[0, 0], fin_recv.at[src, w],
            {"row": src, "col": c - core + w},
        )

    def own_copy(first, count, at):
        span = pl.ds(first, count)
        return describe(own.at[span], theirs.at[span], o_sems, (at,), core_peer)

    def write_out(i):
        swapped = swap_lanes(theirs[i])
        low, high = merge(own[i], swapped), merge(swapped, own[i])
        out_ref[i] = jnp.where(core == 0, low, high)

    def step(i, carry):
        parity = lax.rem(i, 2)

        def deferred(*turns):
            for t in turns:
                later = i + 1 + t
                if t < NEAR:
                    @pl.when(jnp.logical_and(i > 0, later < blocks))
                    def _():
                        lower_step(later, i - 1)
                else:
                    @pl.when(jnp.logical_and(i >= t, i + 2 < blocks))
                    def _():
                        lower_step(i + 2, i - t)

        def places(first, last):
            @pl.when(i == 0)
            def _():
                for t in range(first, last):
                    place(t)

        def residual(a):
            finish(across_copies(i, a))
            total = px[a]
            for s in range(n_x - 1):
                total = total + x_in[parity, a, s]
            turned = [turn(total, d) for d in range(GROUPS)]
            spread = [
                by_group([turned[(g - b) % GROUPS] for g in range(GROUPS)])
                for b in range(GROUPS)
            ]
            eb[a] = halves(jnp.concatenate(spread, axis=0), 1)

        def diag_chunk(a, q):
            rows = span // CHUNKS
            value = product(db[q], eb[a])
            value = by_group([
                value[(h * CORES + v) * rows:(h * CORES + v + 1) * rows]
                for v in range(CORES) for h in range(CHAINS)
            ])
            at = (a * CHUNKS + q) * n_own
            part[at:at + n_own] = value.reshape(n_own, strip, rotor)

        @pl.when(i < blocks - 1)
        def _():
            for a in range(CHAINS):
                residual(a)
                for q in range(CHUNKS):
                    diag_chunk(a, q)
                    for t in range(n_own):
                        @pl.when(owner_away[t])
                        def _():
                            reduce_copy(a * CHUNKS + q, t).start()
            prepare_lower(pair_index(i + 1, i))
            deferred(*range(TURNS))
            places(1, 4)

            @pl.when(is_owner)
            def _():
                for q in range(CHAINS * CHUNKS):
                    at = q * n_own + me_owner
                    total = part[at]
                    for s in range(1, n_row):
                        reduce_arrival(q, s).wait_recv()
                        total = total + rs_in[row_at[s], q]
                    ysh[at] = total
                    for s in reversed(range(1, n_row)):
                        gather_copy(q, s).start()

            deferred(*range(TURNS, blocks - 2))
            places(4, blocks)
            prepare_diag(i + 1)
            for a in range(CHAINS):
                products = []
                for q in range(CHUNKS):
                    at = (a * CHUNKS + q) * n_own
                    for t in range(n_own):
                        @pl.when(owner_away[t])
                        def _():
                            gather_arrival(a * CHUNKS + q, t).wait_recv()
                    ready = halves(ysh[at:at + n_own].reshape(span // CHUNKS, rotor), 1)
                    terms = [product(lb[h, q], ready) for h in range(CHAINS)]
                    products = [p + v for p, v in zip(products, terms)] if q else terms
                send_across(i + 1, a, products)
            chains = [
                ysh[a * strips:(a + 1) * strips].reshape(span, rotor) for a in range(CHAINS)
            ]
            for h in range(CHAINS):
                value = arranged(chains, h)
                whole[h * span:(h + 1) * span] = value
                yd[i, h * span:(h + 1) * span] = halves(value, 1)
            own[i] = whole[pl.ds(r * piece, piece)]
            for q in range(CHAINS * CHUNKS):
                for t in range(n_own):
                    @pl.when(owner_away[t])
                    def _():
                        reduce_copy(q, t).wait_send()

            @pl.when(is_owner)
            def _():
                for q in range(CHAINS * CHUNKS):
                    for s in range(1, n_row):
                        gather_copy(q, s).wait_send()

        @pl.when(i == blocks - 1)
        def _():
            earlier = own_copy(0, blocks - 1, 0)
            earlier.start()
            for a in range(CHAINS):
                residual(a)
                for q in range(CHUNKS):
                    diag_chunk(a, q)
            for g in range(n_row):
                at = g % (n_row // CHAINS) * per_piece
                chains = [
                    part[a * strips + at:a * strips + at + per_piece].reshape(piece, rotor)
                    for a in range(CHAINS)
                ]
                value = arranged(chains, g // (n_row // CHAINS))
                upper, lower_rows = value[:piece // 2], value[piece // 2:]
                last[g, 0] = merge(upper, swap_lanes(lower_rows))
                last[g, 1] = merge(swap_lanes(upper), lower_rows)
                for w in range(CORES):
                    @pl.when(jnp.logical_or(g != r, w != core))
                    def _():
                        final_copy(g, w).start()
            earlier.wait()
            for j in range(blocks - 1):
                write_out(j)
            fin_in[r, core] = last[r, core]
            for s in list(range(1, n_row)) + [0]:
                for w in range(CORES):
                    @pl.when(jnp.logical_or(s != 0, w != core))
                    def _():
                        final_arrival(s, w).wait_recv()
            left, right = (sum(fin_in[g, w] for g in range(n_row)) for w in range(CORES))
            out_ref[blocks - 1, :piece // 2] = merge(left, swap_lanes(right))
            out_ref[blocks - 1, piece // 2:] = merge(swap_lanes(left), right)
            for g in range(n_row):
                for w in range(CORES):
                    @pl.when(jnp.logical_or(g != r, w != core))
                    def _():
                        final_copy(g, w).wait_send()

        return carry

    for a in range(CHAINS):
        send_across(0, a)
    prepare_diag(0)
    lax.fori_loop(0, blocks, step, 0)


def per_device(
    sub_field, reluctivity, stride, counts, source_cell, target_row, lower_tiles, diag_inverse
):
    n_row, n_col = lax.axis_size("row"), lax.axis_size("col")
    blocks, tile_rows, rotor = diag_inverse.shape[0], lower_tiles.shape[1], sub_field.shape[1]
    cap = source_cell.shape[2]
    pairs = lower_tiles.shape[0]
    share = diag_inverse.shape[1]
    piece = share // n_row
    n_x = n_col // CORES
    n_own = n_row // 2
    strips = CHAINS * CHUNKS * n_own
    strip = share // strips
    f32 = jnp.float32
    bf16 = jnp.bfloat16
    vmem = pl.BlockSpec(memory_space=pltpu.VMEM)
    hbm = pl.BlockSpec(memory_space=pltpu.HBM)
    dma = pltpu.SemaphoreType.DMA
    pieces = pl.pallas_call(
        functools.partial(solve_kernel, n_row, n_col),
        out_shape=jax.ShapeDtypeStruct((blocks, piece, rotor), f32),
        in_specs=[pl.BlockSpec(memory_space=pltpu.SMEM)] + [hbm] * 7,
        out_specs=vmem,
        scratch_shapes=[
            pltpu.SMEM(counts.shape, jnp.int32),
            pltpu.SMEM(source_cell.shape, jnp.int32),
            pltpu.VMEM((CORES, n_row, cap), jnp.int32),
            pltpu.VMEM(sub_field.shape, f32),
            pltpu.VMEM(reluctivity.shape, f32),
            pltpu.VMEM((n_row, cap, rotor), f32),
            pltpu.VMEM((n_row, CORES, cap // 2, rotor), f32),
            pltpu.VMEM((n_row * CORES, cap // 2, rotor), f32),
            pltpu.VMEM((n_row * cap, 2 * rotor), bf16),
            pltpu.VMEM((2, tile_rows, n_row * cap), bf16),
            pltpu.VMEM((pairs, CORES) + lower_tiles.shape[1:], f32),
            pltpu.VMEM((blocks, CORES) + diag_inverse.shape[1:], f32),
            pltpu.VMEM((CHAINS, CHUNKS, CORES * tile_rows, 2 * share // CHAINS // CHUNKS), bf16),
            pltpu.VMEM((CHUNKS, CORES * share // CHUNKS, 2 * tile_rows), bf16),
            pltpu.VMEM((blocks, tile_rows, rotor), f32),
            pltpu.VMEM((CHAINS, tile_rows // GROUPS, rotor), f32),
            pltpu.VMEM((2, CHAINS, n_x - 1, tile_rows // GROUPS, rotor), f32),
            pltpu.VMEM((CHAINS, tile_rows, 2 * rotor), bf16),
            pltpu.VMEM((strips, strip, rotor), f32),
            pltpu.VMEM((n_row, CHAINS * CHUNKS, strip, rotor), f32),
            pltpu.VMEM((strips, strip, rotor), f32),
            pltpu.VMEM((blocks, share, 2 * rotor), bf16),
            pltpu.VMEM((share, rotor), f32),
            pltpu.VMEM((n_row, CORES, piece // 2, rotor), f32),
            pltpu.VMEM((n_row, CORES, piece // 2, rotor), f32),
            pltpu.VMEM((blocks, piece, rotor), f32),
            pltpu.VMEM((blocks, piece, rotor), f32),
            dma((5,)),
            dma((2, 1)),
            dma((2, n_row, CORES)),
            dma((pairs,)),
            dma((blocks,)),
            dma((2, pairs)),
            dma((2, blocks)),
            dma((2, 2, CHAINS, n_x - 1)),
            dma((CHAINS * CHUNKS, n_own)),
            dma((n_row, CHAINS * CHUNKS)),
            dma((CHAINS * CHUNKS, n_row - 1)),
            dma((strips,)),
            dma((n_row, CORES)),
            dma((n_row, CORES)),
            dma((2, 1)),
        ],
        compiler_params=pltpu.CompilerParams(
            collective_id=0, has_side_effects=True, vmem_limit_bytes=67043328
        ),
    )(
        stride, counts, source_cell, target_row, sub_field, reluctivity, lower_tiles, diag_inverse
    )
    return pieces[:, None]


def solution(mesh):
    placed = (
        P(("row", "col"), None),
        P(None, ("row", "col"), None),
        P(("row", "col")),
        P(("row", "col"), None),
        P(("row", "col"), None, None),
        P("row", "col", None, None),
        P(None, "row", "col"),
        P(None, "col", "row"),
    )
    return jax.shard_map(
        per_device,
        mesh=mesh,
        in_specs=placed,
        out_specs=P(None, "col", "row", None),
        check_vma=False,
    )
```

```python
import functools

import jax
import jax.numpy as jnp
from jax import lax
from jax.experimental import pallas as pl
from jax.experimental.pallas import tpu as pltpu
from jax.sharding import PartitionSpec as P

MESH = pl.DeviceIdType.MESH
CORES = 2
PICKS = 8
CHAINS = 2
GROUPS = 2 * CHAINS
CHUNKS = 2
DEPTH = 4
TURNS = 0
NEAR = 4


def pair_index(later_block, earlier_block):
    return later_block * (later_block - 1) // 2 + earlier_block


def halves(value, axis):
    high = value.astype(jnp.bfloat16)
    low = (value - high.astype(jnp.float32)).astype(jnp.bfloat16)
    return jnp.concatenate([high, low], axis=axis)


def product(left_halves, right_halves):
    rotor = right_halves.shape[1] // 2
    right = jnp.concatenate([right_halves, right_halves], axis=0)
    full = jnp.dot(left_halves, right, preferred_element_type=jnp.float32)
    return full[:, :rotor] + full[:, rotor:]


def turn(value, groups):
    width = value.shape[1] // GROUPS
    return pltpu.roll(value, groups % GROUPS * width, 1) if groups % GROUPS else value


def group_of(shape):
    return lax.broadcasted_iota(jnp.int32, shape, 1) // (shape[1] // GROUPS)


def by_group(values):
    group = group_of(values[0].shape)

    def among(first, last):
        if last - first == 1:
            return values[first]
        middle = (first + last) // 2
        return jnp.where(group < middle, among(first, middle), among(middle, last))

    return among(0, len(values))


def arranged(chains, part):
    return by_group([turn(chains[g % CHAINS], g % CHAINS - part) for g in range(GROUPS)])


def swap_lanes(value):
    return turn(value, GROUPS // 2)


def solve_kernel(
    n_row, n_col, stride, counts_hbm, source_hbm, target_hbm, field_hbm, nu_hbm, lower_hbm,
    diag_hbm, out_ref, counts, source, target_rows, field, nu, picked, packs, received, arrived, spot,
    lower, diag, lb, db, acc, px, x_in, eb, part, rs_in, ysh, yd, whole, last, fin_in, own, theirs,
    f_sem, t_sems, p_sems, w_sem, d_sem, wr_sems, dr_sems, x_sems, rs_send, rs_recv, ag_send, ag_recv, fin_send,
    fin_recv, o_sems,
):
    blocks, _, share, tile_rows = diag.shape
    rotor = px.shape[2]
    n_x = n_col // CORES
    n_y = n_row // DEPTH
    first_owner, n_own = n_y, n_row // 2
    strip = part.shape[1]
    strips = part.shape[0] // CHAINS
    piece = share // n_row
    per_piece = piece // strip
    r = lax.axis_index("row")
    c = lax.axis_index("col")
    core = lax.rem(c, CORES)
    other = 1 - core
    c_other = c + 1 - 2 * core
    core_peer = {"col": c_other}
    x_peer = [{"col": lax.rem(c + CORES * s, n_col)} for s in range(1, n_x)]
    row_at = [lax.rem(r + s, n_row) for s in range(n_row)]
    cols_at = [c, c_other]
    far_first = sorted(range(1, n_row), key=lambda s: -min(s, n_row - s))
    peers = [{"row": row_at[s], "col": k} for s in far_first for k in cols_at]
    peers += x_peer + [core_peer]
    slots = source.shape[2]
    half_slots = slots // 2
    span = share // CHAINS
    quarter = tile_rows // GROUPS
    is_owner = jnp.logical_and(r >= first_owner, r < first_owner + n_own)
    me_owner = jnp.clip(r - first_owner, 0, n_own - 1)
    owner_at = [lax.rem(r + n_own // 2 + n_own - t, n_own) for t in range(n_own)]
    owner_away = [first_owner + o != r for o in owner_at]

    def first_half(shape):
        return lax.broadcasted_iota(jnp.int32, shape, 1) < rotor // 2

    def merge(left, right):
        return jnp.where(first_half(left.shape), left, right)

    def between(src, dst, send, recv, device):
        return pltpu.make_async_remote_copy(
            src_ref=src, dst_ref=dst, send_sem=send, recv_sem=recv,
            device_id=device, device_id_type=MESH,
        )

    def describe(src, dst, sems, at, device):
        return between(src, dst, sems.at[(0,) + at], sems.at[(1,) + at], device)

    def remote(src, dst, sems, at, device):
        copy = describe(src, dst, sems, at, device)
        copy.start()
        return copy

    def load_lower(k):
        return pltpu.make_async_copy(lower_hbm.at[k], lower.at[k, core], w_sem.at[k])

    def share_lower(k):
        return describe(lower_hbm.at[k], lower.at[k, core], wr_sems, (k,), core_peer)

    def load_diag(k):
        return pltpu.make_async_copy(diag_hbm.at[k], diag.at[k, core], d_sem.at[k])

    def share_diag(k):
        return describe(diag_hbm.at[k], diag.at[k, core], dr_sems, (k,), core_peer)

    def finish(copies):
        for copy in copies:
            copy.wait()

    loads = (
        pltpu.make_async_copy(counts_hbm, counts, f_sem.at[3]),
        pltpu.make_async_copy(source_hbm, source, f_sem.at[4]),
        pltpu.make_async_copy(target_hbm.at[0, 0], target_rows.at[core], f_sem.at[2]),
        pltpu.make_async_copy(field_hbm, field, f_sem.at[0]),
        pltpu.make_async_copy(nu_hbm, nu, f_sem.at[1]),
    )
    barrier = pltpu.get_barrier_semaphore()
    for p in peers:
        pl.semaphore_signal(barrier, inc=1, device_id=p, device_id_type=MESH)
    for copy in loads:
        copy.start()

    def pick(s):
        g = row_at[s]
        band = stride[0]
        live_slots = counts[0, g]

        def group(k8, carry):
            for u in range(PICKS):
                k = k8 * PICKS + u
                m = source[0, g, k]
                here = field[pl.ds(m, 1), :]
                radial = field[pl.ds(jnp.maximum(m - band, 0), 1), :]
                tangent = field[pl.ds(jnp.maximum(m - 1, 0), 1), :]
                has_radial = jnp.where(m >= band, 1.0, 0.0)
                has_tangent = jnp.where(m >= 1, 1.0, 0.0)
                live = jnp.where(k < live_slots, 1.0, 0.0)
                swept = nu[0, pl.ds(m, 1), :] * (here - radial * has_radial) + nu[
                    1, pl.ds(m, 1), :
                ] * (here - tangent * has_tangent)
                picked[s, pl.ds(k, 1), :] = swept * live
            return carry

        lax.fori_loop(0, slots // PICKS, group, 0)
        early, late = picked[s, :half_slots], picked[s, half_slots:]
        packs[s, 0] = merge(early, swap_lanes(late))
        packs[s, 1] = merge(swap_lanes(early), late)

    for copy in loads:
        copy.wait()
    mine = r * CORES + core
    order = [("d", 0)]
    for j in range(blocks - 1):
        order += [("l", pair_index(j + 1, j)), ("d", j + 1)]
        order += [("l", pair_index(i, j)) for i in range(j + 2, blocks)]
    for kind, k in order:
        (load_diag(k) if kind == "d" else load_lower(k)).start()
    sent = []
    for s in list(range(1, n_row)) + [0]:
        pick(s)
        if s == 1:
            pl.semaphore_wait(barrier, len(peers))
            targets_sent = remote(
                target_rows.at[core], target_rows.at[core], t_sems, (0,), core_peer
            )
        for w, (k, col) in enumerate(((core, c), (other, c_other))):
            if s or w:
                sent.append(remote(
                    packs.at[s, k], received.at[mine], p_sems, (s, w), {"row": row_at[s], "col": col},
                ))
    for kind, k in order:
        (share_diag(k) if kind == "d" else share_lower(k)).start()
    received[mine] = packs[0, core]
    targets_sent.wait()
    targets = [
        jnp.concatenate(
            [
                target_rows[k, q:q + 1, h * half_slots:(h + 1) * half_slots]
                for q in range(n_row) for k in range(CORES)
            ],
            axis=1,
        )
        for h in range(2)
    ]

    def chosen(i, h):
        here = lax.broadcasted_iota(jnp.int32, (tile_rows, arrived.shape[0]), 0) + i * tile_rows
        return jnp.where(here == targets[h], 1.0, 0.0).astype(jnp.bfloat16)

    def place(i, rows=None):
        sums = []
        for h in range(2):
            full = jnp.dot(
                rows[h] if rows else chosen(i, h), arrived[...],
                preferred_element_type=jnp.float32,
            )
            sums.append(full[:, :rotor] + full[:, rotor:])
        acc[i] = merge(*sums)

    for h in range(2):
        spot[h] = chosen(0, h)
    finish(sent)
    arrived[...] = halves(received[...].reshape(arrived.shape[0], rotor), 1)
    place(0, [spot[h] for h in range(2)])

    def lower_half(k, h):
        return lower[k, :, :, h * span:(h + 1) * span].reshape(
            CORES * tile_rows, span
        )

    def lower_step(i, j):
        k = pair_index(i, j)
        finish([load_lower(k), share_lower(k)])
        left = halves(lower[k].reshape(CORES * tile_rows, share), 1)
        value = product(left, yd[j])
        acc[i] = acc[i] - merge(value[:tile_rows], value[tile_rows:])

    def prepare_lower(k):
        finish([load_lower(k), share_lower(k)])
        for h in range(CHAINS):
            for q in range(CHUNKS):
                at = slice(q * span // CHUNKS, (q + 1) * span // CHUNKS)
                lb[h, q] = halves(lower_half(k, h)[:, at], 1)

    def prepare_diag(i):
        finish([load_diag(i), share_diag(i)])
        rows = span // CHUNKS
        for q in range(CHUNKS):
            for h in range(CHAINS):
                at = h * span + q * rows
                db[q, h * CORES * rows:(h + 1) * CORES * rows] = halves(
                    diag[i, :, at:at + rows].reshape(CORES * rows, tile_rows), 1
                )

    def across_copies(i, a):
        parity = lax.rem(i, 2)
        return [
            describe(px.at[a], x_in.at[parity, a, s], x_sems, (parity, a, s), p)
            for s, p in enumerate(x_peer)
        ]

    def send_across(i, a, products=None):
        value = acc[i]
        value = jnp.where(lax.rem(group_of(value.shape), CHAINS) == a, value, 0.0)
        if products:
            value = value - by_group([
                products[h][v * tile_rows:(v + 1) * tile_rows]
                for v in range(CORES) for h in range(CHAINS)
            ])
        rows = [value[b * quarter:(b + 1) * quarter] for b in range(GROUPS)]
        px[a] = sum(
            turn(by_group([rows[(g - d) % GROUPS] for g in range(GROUPS)]), -d)
            for d in range(GROUPS)
        )
        for copy in across_copies(i, a):
            copy.start()

    def reduce_copy(q, t):
        o = owner_at[t]
        return between(
            part.at[q * n_own + o], rs_in.at[r, q], rs_send.at[q, t], rs_recv.at[r, q],
            {"row": first_owner + o},
        )

    def reduce_arrival(q, s):
        src = row_at[s]
        return between(
            part.at[q], rs_in.at[src, q], rs_send.at[q, 0], rs_recv.at[src, q], {"row": src}
        )

    def gather_copy(q, s):
        at = q * n_own + me_owner
        return between(
            ysh.at[at], ysh.at[at], ag_send.at[q, s - 1], ag_recv.at[at], {"row": row_at[s]}
        )

    def gather_arrival(q, t):
        at = q * n_own + owner_at[t]
        return between(
            ysh.at[at], ysh.at[at], ag_send.at[q, 0], ag_recv.at[at],
            {"row": first_owner + owner_at[t]},
        )

    def final_copy(g, w):
        return between(
            last.at[g, w], fin_in.at[r, core], fin_send.at[g, w], fin_recv.at[r, core],
            {"row": g, "col": c - core + w},
        )

    def final_arrival(s, w):
        src = row_at[s]
        return between(
            last.at[0, 0], fin_in.at[src, w], fin_send.at[0, 0], fin_recv.at[src, w],
            {"row": src, "col": c - core + w},
        )

    def own_copy(first, count, at):
        span = pl.ds(first, count)
        return describe(own.at[span], theirs.at[span], o_sems, (at,), core_peer)

    def write_out(i):
        swapped = swap_lanes(theirs[i])
        low, high = merge(own[i], swapped), merge(swapped, own[i])
        out_ref[i] = jnp.where(core == 0, low, high)

    def step(i, carry):
        parity = lax.rem(i, 2)

        def deferred(*turns):
            for t in turns:
                later = i + 1 + t
                if t < NEAR:
                    @pl.when(jnp.logical_and(i > 0, later < blocks))
                    def _():
                        lower_step(later, i - 1)
                else:
                    @pl.when(jnp.logical_and(i >= t, i + 2 < blocks))
                    def _():
                        lower_step(i + 2, i - t)

        def places(first, last):
            @pl.when(i == 0)
            def _():
                for t in range(first, last):
                    place(t)

        def residual(a):
            finish(across_copies(i, a))
            total = px[a]
            for s in range(n_x - 1):
                total = total + x_in[parity, a, s]
            turned = [turn(total, d) for d in range(GROUPS)]
            spread = [
                by_group([turned[(g - b) % GROUPS] for g in range(GROUPS)])
                for b in range(GROUPS)
            ]
            eb[a] = halves(jnp.concatenate(spread, axis=0), 1)

        def diag_chunk(a, q):
            rows = span // CHUNKS
            value = product(db[q], eb[a])
            value = by_group([
                value[(h * CORES + v) * rows:(h * CORES + v + 1) * rows]
                for v in range(CORES) for h in range(CHAINS)
            ])
            at = (a * CHUNKS + q) * n_own
            part[at:at + n_own] = value.reshape(n_own, strip, rotor)

        @pl.when(i < blocks - 1)
        def _():
            for a in range(CHAINS):
                residual(a)
                for q in range(CHUNKS):
                    diag_chunk(a, q)
                    for t in range(n_own):
                        @pl.when(owner_away[t])
                        def _():
                            reduce_copy(a * CHUNKS + q, t).start()
            prepare_lower(pair_index(i + 1, i))
            deferred(*range(TURNS))
            places(1, 4)

            @pl.when(is_owner)
            def _():
                for q in range(CHAINS * CHUNKS):
                    at = q * n_own + me_owner
                    total = part[at]
                    for s in range(1, n_row):
                        reduce_arrival(q, s).wait_recv()
                        total = total + rs_in[row_at[s], q]
                    ysh[at] = total
                    for s in reversed(far_first):
                        gather_copy(q, s).start()

            deferred(*range(TURNS, blocks - 2))
            places(4, blocks)
            prepare_diag(i + 1)
            for a in range(CHAINS):
                products = []
                for q in range(CHUNKS):
                    at = (a * CHUNKS + q) * n_own
                    for t in range(n_own):
                        @pl.when(owner_away[t])
                        def _():
                            gather_arrival(a * CHUNKS + q, t).wait_recv()
                    ready = halves(ysh[at:at + n_own].reshape(span // CHUNKS, rotor), 1)
                    terms = [product(lb[h, q], ready) for h in range(CHAINS)]
                    products = [p + v for p, v in zip(products, terms)] if q else terms
                send_across(i + 1, a, products)
            chains = [
                ysh[a * strips:(a + 1) * strips].reshape(span, rotor) for a in range(CHAINS)
            ]
            for h in range(CHAINS):
                value = arranged(chains, h)
                whole[h * span:(h + 1) * span] = value
                yd[i, h * span:(h + 1) * span] = halves(value, 1)
            own[i] = whole[pl.ds(r * piece, piece)]
            for q in range(CHAINS * CHUNKS):
                for t in range(n_own):
                    @pl.when(owner_away[t])
                    def _():
                        reduce_copy(q, t).wait_send()

            @pl.when(is_owner)
            def _():
                for q in range(CHAINS * CHUNKS):
                    for s in range(1, n_row):
                        gather_copy(q, s).wait_send()

        @pl.when(i == blocks - 1)
        def _():
            earlier = own_copy(0, blocks - 1, 0)
            earlier.start()
            for a in range(CHAINS):
                residual(a)
                for q in range(CHUNKS):
                    diag_chunk(a, q)
            for g in range(n_row):
                at = g % (n_row // CHAINS) * per_piece
                chains = [
                    part[a * strips + at:a * strips + at + per_piece].reshape(piece, rotor)
                    for a in range(CHAINS)
                ]
                value = arranged(chains, g // (n_row // CHAINS))
                upper, lower_rows = value[:piece // 2], value[piece // 2:]
                last[g, 0] = merge(upper, swap_lanes(lower_rows))
                last[g, 1] = merge(swap_lanes(upper), lower_rows)
                for w in range(CORES):
                    @pl.when(jnp.logical_or(g != r, w != core))
                    def _():
                        final_copy(g, w).start()
            earlier.wait()
            for j in range(blocks - 1):
                write_out(j)
            fin_in[r, core] = last[r, core]
            for s in list(range(1, n_row)) + [0]:
                for w in range(CORES):
                    @pl.when(jnp.logical_or(s != 0, w != core))
                    def _():
                        final_arrival(s, w).wait_recv()
            left, right = (sum(fin_in[g, w] for g in range(n_row)) for w in range(CORES))
            out_ref[blocks - 1, :piece // 2] = merge(left, swap_lanes(right))
            out_ref[blocks - 1, piece // 2:] = merge(swap_lanes(left), right)
            for g in range(n_row):
                for w in range(CORES):
                    @pl.when(jnp.logical_or(g != r, w != core))
                    def _():
                        final_copy(g, w).wait_send()

        return carry

    for a in range(CHAINS):
        send_across(0, a)
    prepare_diag(0)
    lax.fori_loop(0, blocks, step, 0)


def per_device(
    sub_field, reluctivity, stride, counts, source_cell, target_row, lower_tiles, diag_inverse
):
    n_row, n_col = lax.axis_size("row"), lax.axis_size("col")
    blocks, tile_rows, rotor = diag_inverse.shape[0], lower_tiles.shape[1], sub_field.shape[1]
    cap = source_cell.shape[2]
    pairs = lower_tiles.shape[0]
    share = diag_inverse.shape[1]
    piece = share // n_row
    n_x = n_col // CORES
    n_own = n_row // 2
    strips = CHAINS * CHUNKS * n_own
    strip = share // strips
    f32 = jnp.float32
    bf16 = jnp.bfloat16
    vmem = pl.BlockSpec(memory_space=pltpu.VMEM)
    hbm = pl.BlockSpec(memory_space=pltpu.HBM)
    dma = pltpu.SemaphoreType.DMA
    pieces = pl.pallas_call(
        functools.partial(solve_kernel, n_row, n_col),
        out_shape=jax.ShapeDtypeStruct((blocks, piece, rotor), f32),
        in_specs=[pl.BlockSpec(memory_space=pltpu.SMEM)] + [hbm] * 7,
        out_specs=vmem,
        scratch_shapes=[
            pltpu.SMEM(counts.shape, jnp.int32),
            pltpu.SMEM(source_cell.shape, jnp.int32),
            pltpu.VMEM((CORES, n_row, cap), jnp.int32),
            pltpu.VMEM(sub_field.shape, f32),
            pltpu.VMEM(reluctivity.shape, f32),
            pltpu.VMEM((n_row, cap, rotor), f32),
            pltpu.VMEM((n_row, CORES, cap // 2, rotor), f32),
            pltpu.VMEM((n_row * CORES, cap // 2, rotor), f32),
            pltpu.VMEM((n_row * cap, 2 * rotor), bf16),
            pltpu.VMEM((2, tile_rows, n_row * cap), bf16),
            pltpu.VMEM((pairs, CORES) + lower_tiles.shape[1:], f32),
            pltpu.VMEM((blocks, CORES) + diag_inverse.shape[1:], f32),
            pltpu.VMEM((CHAINS, CHUNKS, CORES * tile_rows, 2 * share // CHAINS // CHUNKS), bf16),
            pltpu.VMEM((CHUNKS, CORES * share // CHUNKS, 2 * tile_rows), bf16),
            pltpu.VMEM((blocks, tile_rows, rotor), f32),
            pltpu.VMEM((CHAINS, tile_rows // GROUPS, rotor), f32),
            pltpu.VMEM((2, CHAINS, n_x - 1, tile_rows // GROUPS, rotor), f32),
            pltpu.VMEM((CHAINS, tile_rows, 2 * rotor), bf16),
            pltpu.VMEM((strips, strip, rotor), f32),
            pltpu.VMEM((n_row, CHAINS * CHUNKS, strip, rotor), f32),
            pltpu.VMEM((strips, strip, rotor), f32),
            pltpu.VMEM((blocks, share, 2 * rotor), bf16),
            pltpu.VMEM((share, rotor), f32),
            pltpu.VMEM((n_row, CORES, piece // 2, rotor), f32),
            pltpu.VMEM((n_row, CORES, piece // 2, rotor), f32),
            pltpu.VMEM((blocks, piece, rotor), f32),
            pltpu.VMEM((blocks, piece, rotor), f32),
            dma((5,)),
            dma((2, 1)),
            dma((2, n_row, CORES)),
            dma((pairs,)),
            dma((blocks,)),
            dma((2, pairs)),
            dma((2, blocks)),
            dma((2, 2, CHAINS, n_x - 1)),
            dma((CHAINS * CHUNKS, n_own)),
            dma((n_row, CHAINS * CHUNKS)),
            dma((CHAINS * CHUNKS, n_row - 1)),
            dma((strips,)),
            dma((n_row, CORES)),
            dma((n_row, CORES)),
            dma((2, 1)),
        ],
        compiler_params=pltpu.CompilerParams(
            collective_id=0, has_side_effects=True, vmem_limit_bytes=67043328
        ),
    )(
        stride, counts, source_cell, target_row, sub_field, reluctivity, lower_tiles, diag_inverse
    )
    return pieces[:, None]


def solution(mesh):
    placed = (
        P(("row", "col"), None),
        P(None, ("row", "col"), None),
        P(("row", "col")),
        P(("row", "col"), None),
        P(("row", "col"), None, None),
        P("row", "col", None, None),
        P(None, "row", "col"),
        P(None, "col", "row"),
    )
    return jax.shard_map(
        per_device,
        mesh=mesh,
        in_specs=placed,
        out_specs=P(None, "col", "row", None),
        check_vma=False,
    )
```
